128 devices in a mesh: segment: 8 (over x, z_lo), ctx: 16 (over z_hi, y, core).
Axes of the slice: x: 4, y: 4, z: 4 (z_hi: 2, z_lo: 2; z = z_hi * 2 + z_lo), core: 2. Of those that a mesh axis runs over, the one named last changes fastest.
Arguments:
- queries: bfloat16 [8, 8, 4096, 2048], P('segment', None, 'ctx'), may hold values from -3 to 3
- keys: bfloat16 [8, 8, 4096, 512], P('segment', None, 'ctx'), may hold values from -3 to 3
- values: bfloat16 [8, 8, 4096, 512], P('segment', None, 'ctx'), may hold values from -6 to 6
- grad_slab: bfloat16 [8, 4096, 2048], P('segment', 'ctx'), may hold values from -6 to 6
- plan: int32 [8], P('segment'), may hold values from 0 to 7
- random_blocks: int32 [32, 3], replicated, may hold values from 1 to 31, as said below
Outputs:
- query_grad: bfloat16 [8, 4096, 2048], P('segment', 'ctx')
- key_grad: bfloat16 [8, 4096, 512], P('segment', 'ctx')
- value_grad: bfloat16 [8, 4096, 512], P('segment', 'ctx')
The draws below stay inside these ranges and needn't reach their ends.
Inputs may be any that keep to these rules, and one draw needn't show every extreme that they name: `random_blocks`: each row b holds 3 different block numbers, none equal to b - 1, b, b + 1 (mod 32) or to 0.
All inputs are finite; a program needn't handle non-finite values.
Results may differ from the reference program's by a relative error of at most 0.012.
Values may be sent and summed in bfloat16 or wider, within the bound.
No kernel may reach another device: no remote copies, remote signals or barrier semaphores. Data moves between devices by JAX's collectives and lax.ppermute only.
A program may use at most 192 MiB of HBM per device.

```python
import jax
import jax.numpy as jnp
from jax import lax

HQ = 16
HK = 4
HD = 128
BLK = 128
NR = 3
MB = 8
SEQ = 4096
NQB = 32
SEGMENTS = 8


def draw_random_blocks(key, part):
    block_ids = jnp.arange(NQB, dtype=jnp.int32)
    row_ids = block_ids[:, None]
    column_ids = block_ids[None, :]
    excluded = (column_ids == row_ids) | (column_ids == (row_ids + 1) % NQB) | (column_ids == (row_ids - 1) % NQB) | (column_ids == 0)
    raw_scores = jax.random.randint(jax.random.fold_in(key, 12), (NQB, NQB), 0, 1 << 16).astype(jnp.int32)
    distinct = raw_scores * NQB + column_ids
    distinct = jnp.where(excluded, -1, distinct)
    top_scores, top_ids = jax.lax.top_k(distinct, NR)
    return top_ids.astype(jnp.int32)


def with_ends(result, key, least, high):
    extent = result.shape
    index_at = [jax.random.randint(jax.random.fold_in(key, axis), (), 0, extent[axis]) for axis in range(len(extent))]
    result = result.at[tuple(index_at)].set(least)
    longest = extent.index(max(extent))
    index_at[longest] = (index_at[longest] + 1) % extent[longest]
    return result.at[tuple(index_at)].set(high)


def block_scale(key, shape, cuts, smallest, top_value):
    loudness = 1.0
    for dim, blocks in cuts:
        heights = jax.random.uniform(jax.random.fold_in(jax.random.fold_in(key, 6), dim), (blocks,), jnp.float32, smallest / len(cuts), top_value / len(cuts))
        loudness = loudness * jnp.repeat(jnp.exp(heights), shape[dim] // blocks).reshape((-1,) + (1,) * (len(shape) - 1 - dim))
    return loudness


def noise(stream_key, extent, scale, reach, cuts=(), kind=jnp.bfloat16):
    array = scale * jax.random.normal(stream_key, extent, jnp.float32)
    if cuts:
        array = array * block_scale(stream_key, extent, cuts, -0.22, 0.18)
    return jnp.clip(array, -reach, reach).astype(kind)


def setup_inputs(seed: int = 0) -> dict:
    key_of = jax.random.split(jax.random.key(seed), 7)
    return {
        "queries": noise(key_of[0], (SEGMENTS, MB, SEQ, HQ * HD), 1.0, 3.0, ((0, 8), (2, 16))),
        "keys": noise(key_of[1], (SEGMENTS, MB, SEQ, HK * HD), 1.0, 3.0, ((0, 8), (2, 16))),
        "values": noise(key_of[2], (SEGMENTS, MB, SEQ, HK * HD), 1.0, 6.0, ((0, 8), (2, 16))),
        "grad_slab": noise(key_of[3], (SEGMENTS, SEQ, HQ * HD), 1.0, 6.0, ((0, 8), (1, 16))),
        "plan": with_ends(jax.random.randint(key_of[4], (SEGMENTS,), 0, MB), jax.random.fold_in(key_of[4], 1), 0, MB - 1).astype(jnp.int32),
        "random_blocks": draw_random_blocks(jax.random.fold_in(key_of[6], 71), 0),
    }


def make_mask(random_blocks):
    block_ids = jnp.arange(NQB, dtype=jnp.int32)
    column_ids = block_ids[None, :]
    row_ids = block_ids[:, None]
    nearby = (column_ids == row_ids) | (column_ids == (row_ids + 1) % NQB) | (column_ids == (row_ids - 1) % NQB)
    chosen = jnp.any(random_blocks[:, :, None] == column_ids[:, None, :], axis=1)
    allowed = nearby | chosen | (column_ids == 0) | (row_ids == 0)
    return allowed.astype(jnp.float32)


def reference(queries, keys, values, grad_slab, plan, random_blocks):
    block_mask = make_mask(random_blocks)
    token_mask = jnp.repeat(jnp.repeat(block_mask, BLK, axis=0), BLK, axis=1)
    score_scale = HD ** -0.5
    group_size = HQ // HK

    def one_segment(segment_id):
        chosen_mb = plan[segment_id]
        query_all = queries[segment_id, chosen_mb]
        key_all = keys[segment_id, chosen_mb]
        value_all = values[segment_id, chosen_mb]
        upstream = grad_slab[(segment_id + 1) % SEGMENTS]

        def one_head(head_id):
            kv_head = head_id // group_size
            head_query = lax.dynamic_slice_in_dim(query_all, head_id * HD, HD, 1)
            head_grad = lax.dynamic_slice_in_dim(upstream, head_id * HD, HD, 1)
            head_key = lax.dynamic_slice_in_dim(key_all, kv_head * HD, HD, 1)
            head_value = lax.dynamic_slice_in_dim(value_all, kv_head * HD, HD, 1)
            scores = jnp.dot(head_query, head_key.T, preferred_element_type=jnp.float32) * score_scale
            exp_scores = jnp.exp(scores) * token_mask
            totals = jnp.sum(exp_scores, axis=1)
            weights = exp_scores / totals[:, None]
            weights_low = weights.astype(jnp.bfloat16)
            dprobs = jnp.dot(head_grad, head_value.T, preferred_element_type=jnp.float32)
            deltas = jnp.sum(weights_low.astype(jnp.float32) * dprobs, axis=1)
            dscore = (weights * (dprobs - deltas[:, None])).astype(jnp.bfloat16)
            dquery = score_scale * jnp.dot(dscore, head_key, preferred_element_type=jnp.float32)
            key_term = score_scale * jnp.dot(dscore.T, head_query, preferred_element_type=jnp.float32)
            value_term = jnp.dot(weights_low.T, head_grad, preferred_element_type=jnp.float32)
            return dquery, key_term, value_term

        dquery, key_term, value_term = lax.map(one_head, jnp.arange(HQ, dtype=jnp.int32))
        query_out = dquery.transpose(1, 0, 2).reshape(SEQ, HQ * HD).astype(jnp.bfloat16)
        key_out = key_term.reshape(HK, group_size, SEQ, HD).sum(axis=1).transpose(1, 0, 2).reshape(SEQ, HK * HD)
        value_out = value_term.reshape(HK, group_size, SEQ, HD).sum(axis=1).transpose(1, 0, 2).reshape(SEQ, HK * HD)
        return query_out, key_out.astype(jnp.bfloat16), value_out.astype(jnp.bfloat16)

    query_grad, key_grad, value_grad = lax.map(one_segment, jnp.arange(SEGMENTS, dtype=jnp.int32))
    return (query_grad, key_grad, value_grad)
```

```python
import functools
import math

import jax
import jax.numpy as jnp
from jax import lax
from jax.experimental import pallas as pl
from jax.experimental.pallas import tpu as pltpu
from jax.sharding import PartitionSpec as P

HD = 128
BLK = 128
NH = 4
SCALE = HD**-0.5
EXP2_SCALE = SCALE * math.log2(math.e)
F32 = jnp.float32
BF16 = jnp.bfloat16
NT = (((1,), (1,)), ((), ()))
TN = (((0,), (0,)), ((), ()))
MIB = 2**20


def dot(a, b, dims=(((1,), (0,)), ((), ()))):
    return lax.dot_general(a, b, dims, preferred_element_type=F32)


def params(mib=8):
    return pltpu.CompilerParams(vmem_limit_bytes=mib * MIB)


def on_chip(kernel, name, out_shape, *operands, scratch=(), mib=8):
    vmem = pl.BlockSpec(memory_space=pltpu.VMEM)
    return pl.pallas_call(
        kernel,
        in_specs=[pl.BlockSpec(memory_space=pltpu.SMEM)] + [vmem] * (len(operands) - 1),
        out_specs=[vmem] * len(out_shape),
        out_shape=out_shape,
        scratch_shapes=list(scratch),
        compiler_params=params(mib),
        name=name,
    )(*operands)


def shape(dims, dtype):
    return jax.ShapeDtypeStruct(dims, dtype)


def stored(dims, dtype):
    return pltpu.HBM(dims, dtype)


def after(x, *others):
    return lax.optimization_barrier((x, *others))[0]


def pack_kernel(
    info_ref, k_ref, v_ref, q_ref, g_ref,
    kv_ref, send_ref, edge_ref, q0_ref, q1_ref, g0_ref, g1_ref,
):
    edge = pl.ds(pl.multiple_of(info_ref[1] % 2 * BLK, BLK), BLK)
    for i, ref in enumerate((k_ref, v_ref)):
        kv_ref[i] = ref[0]
        edge_ref[i] = ref[0, edge, :]
        for b in range(2):
            for j in range(8):
                piece = ref[0, b * BLK + j * 16 : b * BLK + (j + 1) * 16, :]
                send_ref[j, i, b] = piece
                send_ref[j + 8, i, b] = piece
    half = q0_ref.shape[1]
    q0_ref[...] = q_ref[0, :, :half]
    q1_ref[...] = q_ref[0, :, half:]
    g0_ref[...] = g_ref[:, :half]
    g1_ref[...] = g_ref[:, half:]


def pack(info, keys, values, queries, grad):
    width, q_width = keys.shape[2], queries.shape[2]
    spec = pl.BlockSpec((1, 2 * BLK, width), lambda i, info: (info[0], 0, 0))
    half = pl.BlockSpec((BLK, q_width // 2), lambda i, info: (0, 0))
    inputs = [pltpu.with_memory_space_constraint(a, pltpu.HBM) for a in (keys, values, queries, grad)]
    return pl.pallas_call(
        pack_kernel,
        grid_spec=pltpu.PrefetchScalarGridSpec(
            num_scalar_prefetch=1,
            grid=(1,),
            in_specs=[
                spec,
                spec,
                pl.BlockSpec((1, BLK, q_width), lambda i, info: (info[0], 0, 0)),
                pl.BlockSpec((BLK, q_width), lambda i, info: (0, 0)),
            ],
            out_specs=[
                pl.BlockSpec((2, 2 * BLK, width), lambda i, info: (0, 0, 0)),
                pl.BlockSpec((16, 2, 2, 16, width), lambda i, info: (0, 0, 0, 0, 0)),
                pl.BlockSpec((2, BLK, width), lambda i, info: (0, 0, 0)),
                *[half] * 4,
            ],
        ),
        out_shape=[
            stored((2, 2 * BLK, width), BF16),
            stored((16, 2, 2, 16, width), BF16),
            stored((2, BLK, width), BF16),
            *[stored((BLK, q_width // 2), BF16)] * 4,
        ],
        compiler_params=params(16),
        name="pack",
    )(info, *inputs)


def select_kernel(table_ref, got_ref, send_ref):
    for d in range(8):
        for s in range(7):
            block = table_ref[d * 7 + s]
            owner, which = block // 2, block % 2
            for i in range(2):
                send_ref[d, i, s] = got_ref[owner, i, which]


def combine_kernel(table_ref, got_ref, row_ref, send_ref, acc_ref):
    acc_ref[...] = jnp.zeros_like(acc_ref)
    acc_ref[:, :, :, :, columns(table_ref[56], 2 * HD)] = row_ref[...]
    for d in range(8):
        for s in range(7):
            block = table_ref[d * 7 + s]
            owner, which = block // 2, block % 2
            for i in range(2):
                acc_ref[owner, i, which] += got_ref[d, i, s].astype(F32)
    send_ref[...] = acc_ref[...].astype(BF16)


def heads_to_rows(cols):
    return jnp.concatenate([cols[:, h * HD : (h + 1) * HD] for h in range(NH)], axis=0)


def columns(g, width):
    return pl.ds(pl.multiple_of(g * width, width), width)


def attend_kernel(
    info_ref, q_ref, do_ref, own_ref, part_ref, nb_ref, rv_ref,
    dq_ref, down_ref, winp_ref, winn_ref, send_ref, wk_ref, zero_ref,
):
    rank = info_ref[1]
    even = rank % 2 == 0

    @pl.when(even)
    def _():
        wk_ref[0] = nb_ref[...]
        wk_ref[1] = part_ref[:, :BLK, :]

    @pl.when(jnp.logical_not(even))
    def _():
        wk_ref[0] = part_ref[:, BLK:, :]
        wk_ref[1] = nb_ref[...]

    def attend(n):
        rows = slice(n * BLK, (n + 1) * BLK)
        q, do = heads_to_rows(q_ref[0, rows, :]), heads_to_rows(do_ref[rows, :])

        def blocks(i):
            parts = [own_ref[i], wk_ref[n, i], rv_ref[:, i, 0].reshape(BLK, HD)]
            parts += [rv_ref[:, i, 1 + 3 * n + j].reshape(BLK, HD) for j in range(3)]
            return jnp.concatenate(parts, axis=0)

        k, v = blocks(0), blocks(1)
        e = jnp.exp2(dot(k, q, NT) * EXP2_SCALE)
        if n == 1:
            twice = jnp.logical_or(rank == 0, rank == 15)
            keep = jnp.where(twice, 0.0, 1.0).astype(F32)
            e = jnp.concatenate([e[: 3 * BLK], e[3 * BLK : 4 * BLK] * keep, e[4 * BLK :]], axis=0)
        p = e * (1.0 / jnp.sum(e, axis=0, keepdims=True))
        pb = p.astype(BF16)
        dp = dot(v, do, NT)
        delta = jnp.sum(p * dp, axis=0, keepdims=True)
        ds = (p * (dp - delta)).astype(BF16)
        dqt = dot(k, ds, TN) * SCALE
        dq_ref[rows, :] = jnp.concatenate(
            [dqt[:, h * HD : (h + 1) * HD].T for h in range(NH)], axis=1
        ).astype(BF16)
        return dot(ds, q) * SCALE, dot(pb, do)

    def emit(n, grads):
        for i, grad in enumerate(grads):
            if n == 0:
                down_ref[i] = grad[: 2 * BLK]
                zero_ref[i] = grad[3 * BLK : 4 * BLK]
            else:
                down_ref[i] += grad[: 2 * BLK]
                total = zero_ref[i] + grad[3 * BLK : 4 * BLK]
                send_ref[:, i, 0] = total.astype(BF16).reshape(8, 16, HD)
            wk_ref[n, i] = grad[2 * BLK : 3 * BLK].astype(BF16)
            for j in range(3):
                got = grad[(4 + j) * BLK : (5 + j) * BLK].astype(BF16)
                send_ref[:, i, 1 + 3 * n + j] = got.reshape(8, 16, HD)

    @pl.when(rank != 0)
    def _():
        emit(0, attend(0))

    @pl.when(rank == 0)
    def _():
        dq_ref[:BLK, :] = jnp.zeros((BLK, NH * HD), BF16)
        emit(0, [jnp.zeros((7 * BLK, HD), F32)] * 2)

    emit(1, attend(1))

    @pl.when(even)
    def _():
        winn_ref[...] = wk_ref[0]
        winp_ref[...] = wk_ref[1]

    @pl.when(jnp.logical_not(even))
    def _():
        winp_ref[...] = wk_ref[0]
        winn_ref[...] = wk_ref[1]


def attend(info, queries, upstream, own, partner, neighbour, got):
    q_width, width = queries.shape[2], own.shape[2]
    kv_spec = pl.BlockSpec((2, 2 * BLK, HD), lambda g, info: (0, 0, g))
    win_spec = pl.BlockSpec((2, BLK, HD), lambda g, info: (0, 0, g))
    piece_spec = pl.BlockSpec((8, 2, 7, 16, HD), lambda g, info: (0, 0, 0, 0, g))
    row_spec = pl.BlockSpec((2 * BLK, NH * HD), lambda g, info: (0, g))
    return pl.pallas_call(
        attend_kernel,
        grid_spec=pltpu.PrefetchScalarGridSpec(
            num_scalar_prefetch=1,
            grid=(width // HD,),
            in_specs=[
                pl.BlockSpec((1, 2 * BLK, NH * HD), lambda g, info: (info[0], 0, g)),
                row_spec, kv_spec, kv_spec, win_spec, piece_spec,
            ],
            out_specs=[row_spec, kv_spec, win_spec, win_spec, piece_spec],
            scratch_shapes=[pltpu.VMEM((2, 2, BLK, HD), BF16), pltpu.VMEM((2, BLK, HD), F32)],
        ),
        out_shape=[
            stored((2 * BLK, q_width), BF16),
            stored((2, 2 * BLK, width), F32),
            stored((2, BLK, width), BF16),
            stored((2, BLK, width), BF16),
            stored((8, 2, 7, 16, width), BF16),
        ],
        compiler_params=params(28),
        cost_estimate=pl.CostEstimate(
            flops=10 * q_width * 14 * BLK * BLK, transcendentals=q_width * 14 * BLK, bytes_accessed=10 * MIB
        ),
        name="attend",
    )(
        info,
        *(
            pltpu.with_memory_space_constraint(a, pltpu.HBM)
            for a in (queries, upstream, own, partner, neighbour)
        ),
        got,
    )


def row_parts(info_ref, x_ref, got_ref, g):
    kc = columns(2 * (info_ref[1] // 8) + g, HD)
    qc = slice(g * NH * HD, (g + 1) * NH * HD)
    n_keys = got_ref.shape[0] * 2 * 16
    q, do = heads_to_rows(x_ref[0, :, qc]), heads_to_rows(x_ref[1, :, qc])
    return (q, do, *(got_ref[:, i, :, :, kc].reshape(n_keys, HD) for i in range(2)))


def stats_kernel(info_ref, x_ref, got_ref, out_ref):
    for g in range(2):
        q, do, k, v = row_parts(info_ref, x_ref, got_ref, g)
        e = jnp.exp2(dot(k, q, NT) * EXP2_SCALE)
        total = jnp.sum(e, axis=0, keepdims=True)
        inverse = jnp.where(total > 0, 1.0 / total, 0.0)
        delta = jnp.sum(e * inverse * dot(v, do, NT), axis=0, keepdims=True)
        rows = [a[:, h * BLK : (h + 1) * BLK] for a in (total, delta) for h in range(NH)]
        out_ref[g] = jnp.concatenate(rows, axis=0)


def row_kernel(info_ref, x_ref, got_ref, st_ref, dq_ref, down_ref):
    def lanes(a):
        return jnp.concatenate([a[h : h + 1] for h in range(NH)], axis=1)

    for g in range(2):
        q, do, k, v = row_parts(info_ref, x_ref, got_ref, g)
        inverse, mixed = 1.0 / st_ref[g, :NH, :], st_ref[g, NH:, :]
        p = jnp.exp2(dot(k, q, NT) * EXP2_SCALE) * lanes(inverse)
        pb = p.astype(BF16)
        ds = (p * (dot(v, do, NT) - lanes(mixed))).astype(BF16)
        dqt = dot(k, ds, TN) * SCALE
        dq_ref[:, g * NH * HD : (g + 1) * NH * HD] = jnp.concatenate(
            [dqt[:, h * HD : (h + 1) * HD].T for h in range(NH)], axis=1
        ).astype(BF16)
        kc = slice(g * HD, (g + 1) * HD)
        for i, grad in enumerate((dot(ds, q) * SCALE, dot(pb, do))):
            down_ref[:, i, :, :, kc] = grad.reshape(16, 2, 16, HD)


def place_kernel(info_ref, *refs):
    *part_refs, dq_ref, out_ref = refs
    width = part_refs[0].shape[1]

    @pl.when(info_ref[1] == 0)
    def _():
        for h in range(2):
            out_ref[:, h * width : (h + 1) * width] = part_refs[h][...]

    @pl.when(info_ref[1] != 0)
    def _():
        out_ref[...] = dq_ref[...]


def place(info, parts, dq):
    top = pl.BlockSpec((BLK, dq.shape[1]), lambda i, info: (0, 0))
    piece = pl.BlockSpec(parts[0].shape, lambda i, info: (0, 0))
    return pl.pallas_call(
        place_kernel,
        grid_spec=pltpu.PrefetchScalarGridSpec(
            num_scalar_prefetch=1, grid=(1,), in_specs=[piece] * 2 + [top], out_specs=top
        ),
        out_shape=stored(dq.shape, BF16),
        input_output_aliases={3: 0},
        compiler_params=params(12),
        name="place",
    )(info, *parts, dq)


def finish_kernel(info_ref, own_ref, winp_ref, winn_ref, got_ref, dk_ref, dv_ref):
    even = info_ref[1] % 2 == 0

    def total(first_ref, second_ref):
        for i, out_ref in enumerate((dk_ref, dv_ref)):
            for b, win_ref in enumerate((first_ref, second_ref)):
                for j in range(8):
                    rows = slice(b * BLK + j * 16, b * BLK + (j + 1) * 16)
                    pieces = got_ref[j, i, b].astype(F32) + got_ref[j + 8, i, b].astype(F32)
                    window = win_ref[i, j * 16 : (j + 1) * 16].astype(F32)
                    out_ref[rows, :] = (own_ref[i, rows, :] + pieces + window).astype(BF16)

    @pl.when(even)
    def _():
        total(winn_ref, winp_ref)

    @pl.when(jnp.logical_not(even))
    def _():
        total(winp_ref, winn_ref)


def send(block, pairs):
    return lax.ppermute(block, "ctx", pairs)


def add(a, *others):
    total = a.astype(F32)
    for o in others:
        total = total + o.astype(F32)
    return total.astype(BF16)


def merge_stats(mine, other):
    sums, deltas = zip(*((a[:, :NH], a[:, NH:]) for a in (mine, other)))
    total = sums[0] + sums[1]
    inverse = jnp.where(total > 0, 1.0 / total, 0.0)
    delta = (sums[0] * inverse) * deltas[0] + (sums[1] * inverse) * deltas[1]
    return jnp.concatenate([total, delta], axis=1)


def per_device(queries, keys, values, grad_slab, plan, random_blocks):
    n_seg, n_ctx = lax.axis_size("segment"), lax.axis_size("ctx")
    rank = lax.axis_index("ctx").astype(jnp.int32)
    queries, keys, values, grad = queries[0], keys[0], values[0], grad_slab[0]
    width, q_width = keys.shape[2], queries.shape[2]
    half = q_width // 2
    info = jnp.concatenate([plan, rank[None]])
    halves = [list(range(8)), list(range(8, 16))]
    slots = jnp.concatenate(
        [jnp.zeros((n_ctx, 1), jnp.int32), random_blocks.reshape(n_ctx, 6)], axis=1
    )
    side = rank // 8
    table = lax.dynamic_slice_in_dim(slots, side * 8, 8, 0).reshape(56)
    table = jnp.concatenate([table, side[None]])

    def exchange(x):
        return lax.all_to_all(x, "ctx", 0, 0, tiled=True)

    def exchange_half(x):
        return lax.all_to_all(x, "ctx", 0, 0, tiled=True, axis_index_groups=halves)

    both = ("segment", "ctx")

    def flat(s, r):
        return (s % n_seg) * n_ctx + r

    own, send1, edge, q0, q1, g0, g1 = pack(info, keys, values, queries, grad)
    q1 = send(q1, [(0, 8)])
    g0 = lax.ppermute(g0, both, [(flat(s + 1, 0), flat(s, 0)) for s in range(n_seg)])
    g1 = lax.ppermute(g1, both, [(flat(s + 1, 0), flat(s, 8)) for s in range(n_seg)])
    got1 = exchange(send1)
    x = jnp.stack([jnp.where(rank == 0, q0, jnp.zeros((), BF16)) + q1, g0 + g1])
    swap = [(r, r ^ 1) for r in range(n_ctx)]
    ring = [(r, (r - 1 if r % 2 == 0 else r + 1) % n_ctx) for r in range(n_ctx)]
    partner, neighbour = send(own, swap), send(edge, ring)
    x = x + sum(send(x, [(r, r + 2 * y) for r in (0, 8)]) for y in (1, 2, 3))
    x, got1, grad, partner, neighbour = lax.optimization_barrier(
        (x, got1, grad, partner, neighbour)
    )
    upstream = lax.ppermute(grad, "segment", [((s + 1) % n_seg, s) for s in range(n_seg)])
    (send2,) = on_chip(select_kernel, "select", [stored((8, 2, 7, 16, width), BF16)], table, got1)
    got2 = exchange_half(send2)
    x = x + send(x, [(r, r + 1) for r in range(0, n_ctx, 2)])
    (stats,) = on_chip(stats_kernel, "row_stats", [stored((2, 8, BLK), F32)], info, x, got1)
    stats = merge_stats(stats, send(stats, swap))
    others = [
        send(stats, [(r, (r // 8) * 8 + (r + 2 * y) % 8) for r in range(n_ctx)]) for y in (1, 2, 3)
    ]
    got2, stats, *others = lax.optimization_barrier((got2, stats, *others))
    dq, down, winp, winn, send3 = attend(
        info, queries, upstream, own, partner, neighbour, got2
    )
    got3 = exchange_half(send3)
    stats, *others = lax.optimization_barrier((stats, *others, send3))[:4]
    stats = merge_stats(merge_stats(stats, others[1]), merge_stats(others[0], others[2]))
    part, row = on_chip(
        row_kernel,
        "row_grads",
        [stored((BLK, half), BF16), stored((16, 2, 2, 16, 2 * HD), F32)],
        info, x, got1, stats,
    )
    winp, winn = send(winp, swap), send(winn, ring)
    part = add(part, send(part, [(r + 1, r) for r in range(0, n_ctx, 2)]))
    near = [send(part, [(r + 2 * y, r) for r in (0, 8)]) for y in (1, 2, 3)]
    got3, winp, part, *near = lax.optimization_barrier((got3, winp, part, *near))

    (send4,) = on_chip(
        combine_kernel,
        "combine",
        [stored((16, 2, 2, 16, width), BF16)],
        table, got3, row,
        scratch=[pltpu.VMEM((16, 2, 2, 16, width), F32)],
    )
    got4 = exchange(send4)
    part = after(add(part, *near), send4)
    dq = place(info, [part, send(part, [(8, 0)])], dq)
    got4, dq = lax.optimization_barrier((got4, dq))
    dk, dv = on_chip(
        finish_kernel,
        "finish",
        [shape((2 * BLK, width), BF16)] * 2,
        info, down, winp, winn, got4,
    )
    return dq[None], dk[None], dv[None]


def solution(mesh):
    return jax.shard_map(
        per_device,
        mesh=mesh,
        in_specs=(
            P("segment", None, "ctx", None),
            P("segment", None, "ctx", None),
            P("segment", None, "ctx", None),
            P("segment", "ctx", None),
            P("segment"),
            P(),
        ),
        out_specs=(P("segment", "ctx", None), P("segment", "ctx", None), P("segment", "ctx", None)),
        check_vma=False,
    )
```

```python
import functools
import math

import jax
import jax.numpy as jnp
from jax import lax
from jax.experimental import pallas as pl
from jax.experimental.pallas import tpu as pltpu
from jax.sharding import PartitionSpec as P

HD = 128
BLK = 128
NH = 4
SCALE = HD**-0.5
EXP2_SCALE = SCALE * math.log2(math.e)
F32 = jnp.float32
BF16 = jnp.bfloat16
NT = (((1,), (1,)), ((), ()))
TN = (((0,), (0,)), ((), ()))
MIB = 2**20


def dot(a, b, dims=(((1,), (0,)), ((), ()))):
    return lax.dot_general(a, b, dims, preferred_element_type=F32)


def params(mib=8):
    return pltpu.CompilerParams(vmem_limit_bytes=mib * MIB)


def on_chip(kernel, name, out_shape, *operands, scratch=(), mib=8):
    vmem = pl.BlockSpec(memory_space=pltpu.VMEM)
    return pl.pallas_call(
        kernel,
        in_specs=[pl.BlockSpec(memory_space=pltpu.SMEM)] + [vmem] * (len(operands) - 1),
        out_specs=[vmem] * len(out_shape),
        out_shape=out_shape,
        scratch_shapes=list(scratch),
        compiler_params=params(mib),
        name=name,
    )(*operands)


def shape(dims, dtype):
    return jax.ShapeDtypeStruct(dims, dtype)


def stored(dims, dtype):
    return pltpu.HBM(dims, dtype)


def after(x, *others):
    return lax.optimization_barrier((x, *others))[0]


def pack_kernel(
    info_ref, k_ref, v_ref, q_ref, g_ref,
    kv_ref, send_ref, edge_ref, q0_ref, q1_ref, g0_ref, g1_ref,
):
    edge = pl.ds(pl.multiple_of(info_ref[1] % 2 * BLK, BLK), BLK)
    for i, ref in enumerate((k_ref, v_ref)):
        kv_ref[i] = ref[0]
        edge_ref[i] = ref[0, edge, :]
        for b in range(2):
            for j in range(8):
                piece = ref[0, b * BLK + j * 16 : b * BLK + (j + 1) * 16, :]
                send_ref[j, i, b] = piece
                send_ref[j + 8, i, b] = piece
    half = q0_ref.shape[1]
    q0_ref[...] = q_ref[0, :, :half]
    q1_ref[...] = q_ref[0, :, half:]
    g0_ref[...] = g_ref[:, :half]
    g1_ref[...] = g_ref[:, half:]


def pack(info, keys, values, queries, grad):
    width, q_width = keys.shape[2], queries.shape[2]
    spec = pl.BlockSpec((1, 2 * BLK, width), lambda i, info: (info[0], 0, 0))
    half = pl.BlockSpec((BLK, q_width // 2), lambda i, info: (0, 0))
    inputs = [pltpu.with_memory_space_constraint(a, pltpu.HBM) for a in (keys, values, queries, grad)]
    return pl.pallas_call(
        pack_kernel,
        grid_spec=pltpu.PrefetchScalarGridSpec(
            num_scalar_prefetch=1,
            grid=(1,),
            in_specs=[
                spec,
                spec,
                pl.BlockSpec((1, BLK, q_width), lambda i, info: (info[0], 0, 0)),
                pl.BlockSpec((BLK, q_width), lambda i, info: (0, 0)),
            ],
            out_specs=[
                pl.BlockSpec((2, 2 * BLK, width), lambda i, info: (0, 0, 0)),
                pl.BlockSpec((16, 2, 2, 16, width), lambda i, info: (0, 0, 0, 0, 0)),
                pl.BlockSpec((2, BLK, width), lambda i, info: (0, 0, 0)),
                *[half] * 4,
            ],
        ),
        out_shape=[
            stored((2, 2 * BLK, width), BF16),
            stored((16, 2, 2, 16, width), BF16),
            stored((2, BLK, width), BF16),
            *[stored((BLK, q_width // 2), BF16)] * 4,
        ],
        compiler_params=params(16),
        name="pack",
    )(info, *inputs)


def select_kernel(table_ref, got_ref, send_ref):
    for d in range(8):
        for s in range(7):
            block = table_ref[d * 7 + s]
            owner, which = block // 2, block % 2
            for i in range(2):
                send_ref[d, i, s] = got_ref[owner, i, which]


def combine_kernel(table_ref, got_ref, row_ref, send_ref, acc_ref):
    acc_ref[...] = jnp.zeros_like(acc_ref)
    acc_ref[:, :, :, :, columns(table_ref[56], 2 * HD)] = row_ref[...]
    for d in range(8):
        for s in range(7):
            block = table_ref[d * 7 + s]
            owner, which = block // 2, block % 2
            for i in range(2):
                acc_ref[owner, i, which] += got_ref[d, i, s].astype(F32)
    send_ref[...] = acc_ref[...].astype(BF16)


def heads_to_rows(cols):
    return jnp.concatenate([cols[:, h * HD : (h + 1) * HD] for h in range(NH)], axis=0)


def columns(g, width):
    return pl.ds(pl.multiple_of(g * width, width), width)


def attend_kernel(
    info_ref, q_ref, do_ref, own_ref, part_ref, nb_ref, rv_ref,
    dq_ref, down_ref, winp_ref, winn_ref, send_ref, wk_ref, zero_ref,
):
    rank = info_ref[1]
    even = rank % 2 == 0

    @pl.when(even)
    def _():
        wk_ref[0] = nb_ref[...]
        wk_ref[1] = part_ref[:, :BLK, :]

    @pl.when(jnp.logical_not(even))
    def _():
        wk_ref[0] = part_ref[:, BLK:, :]
        wk_ref[1] = nb_ref[...]

    def operands(n):
        rows = slice(n * BLK, (n + 1) * BLK)
        q, do = heads_to_rows(q_ref[0, rows, :]), heads_to_rows(do_ref[rows, :])

        def blocks(i):
            parts = [own_ref[i], wk_ref[n, i], rv_ref[:, i, 0].reshape(BLK, HD)]
            parts += [rv_ref[:, i, 1 + 3 * n + j].reshape(BLK, HD) for j in range(3)]
            return jnp.concatenate(parts, axis=0)

        return q, do, blocks(0), blocks(1)

    def exp_scores(n, q, do, k, v):
        e = jnp.exp2(dot(k, q, NT) * EXP2_SCALE)
        if n == 1:
            twice = jnp.logical_or(rank == 0, rank == 15)
            keep = jnp.where(twice, 0.0, 1.0).astype(F32)
            e = jnp.concatenate([e[: 3 * BLK], e[3 * BLK : 4 * BLK] * keep, e[4 * BLK :]], axis=0)
        return e

    def weights(e, q, do, k, v):
        p = e * (1.0 / jnp.sum(e, axis=0, keepdims=True))
        dp = dot(v, do, NT)
        delta = jnp.sum(p * dp, axis=0, keepdims=True)
        return p.astype(BF16), (p * (dp - delta)).astype(BF16)

    def grads(n, pb, ds, q, do, k, v):
        dqt = dot(k, ds, TN) * SCALE
        dq_ref[n * BLK : (n + 1) * BLK, :] = jnp.concatenate(
            [dqt[:, h * HD : (h + 1) * HD].T for h in range(NH)], axis=1
        ).astype(BF16)
        return dot(ds, q) * SCALE, dot(pb, do)

    def emit(n, grads):
        for i, grad in enumerate(grads):
            if n == 0:
                down_ref[i] = grad[: 2 * BLK]
                zero_ref[i] = grad[3 * BLK : 4 * BLK]
            else:
                down_ref[i] += grad[: 2 * BLK]
                total = zero_ref[i] + grad[3 * BLK : 4 * BLK]
                send_ref[:, i, 0] = total.astype(BF16).reshape(8, 16, HD)
            wk_ref[n, i] = grad[2 * BLK : 3 * BLK].astype(BF16)
            for j in range(3):
                got = grad[(4 + j) * BLK : (5 + j) * BLK].astype(BF16)
                send_ref[:, i, 1 + 3 * n + j] = got.reshape(8, 16, HD)

    given = [operands(n) for n in range(2)]
    scores = [exp_scores(n, *given[n]) for n in range(2)]
    shares = [weights(scores[n], *given[n]) for n in range(2)]
    first, second = (grads(n, *shares[n], *given[n]) for n in range(2))
    emit(0, [jnp.where(rank != 0, term, 0.0) for term in first])
    emit(1, second)

    @pl.when(even)
    def _():
        winn_ref[...] = wk_ref[0]
        winp_ref[...] = wk_ref[1]

    @pl.when(jnp.logical_not(even))
    def _():
        winp_ref[...] = wk_ref[0]
        winn_ref[...] = wk_ref[1]


def attend(info, queries, upstream, own, partner, neighbour, got):
    q_width, width = queries.shape[2], own.shape[2]
    kv_spec = pl.BlockSpec((2, 2 * BLK, HD), lambda g, info: (0, 0, g))
    win_spec = pl.BlockSpec((2, BLK, HD), lambda g, info: (0, 0, g))
    piece_spec = pl.BlockSpec((8, 2, 7, 16, HD), lambda g, info: (0, 0, 0, 0, g))
    row_spec = pl.BlockSpec((2 * BLK, NH * HD), lambda g, info: (0, g))
    return pl.pallas_call(
        attend_kernel,
        grid_spec=pltpu.PrefetchScalarGridSpec(
            num_scalar_prefetch=1,
            grid=(width // HD,),
            in_specs=[
                pl.BlockSpec((1, 2 * BLK, NH * HD), lambda g, info: (info[0], 0, g)),
                row_spec, kv_spec, kv_spec, win_spec, piece_spec,
            ],
            out_specs=[row_spec, kv_spec, win_spec, win_spec, piece_spec],
            scratch_shapes=[pltpu.VMEM((2, 2, BLK, HD), BF16), pltpu.VMEM((2, BLK, HD), F32)],
        ),
        out_shape=[
            stored((2 * BLK, q_width), BF16),
            stored((2, 2 * BLK, width), F32),
            stored((2, BLK, width), BF16),
            stored((2, BLK, width), BF16),
            stored((8, 2, 7, 16, width), BF16),
        ],
        compiler_params=params(28),
        cost_estimate=pl.CostEstimate(
            flops=10 * q_width * 14 * BLK * BLK, transcendentals=q_width * 14 * BLK, bytes_accessed=10 * MIB
        ),
        name="attend",
    )(
        info,
        *(
            pltpu.with_memory_space_constraint(a, pltpu.HBM)
            for a in (queries, upstream, own, partner, neighbour)
        ),
        got,
    )


def row_parts(info_ref, x_ref, got_ref, g):
    kc = columns(2 * (info_ref[1] // 8) + g, HD)
    qc = slice(g * NH * HD, (g + 1) * NH * HD)
    n_keys = got_ref.shape[0] * 2 * 16
    q, do = heads_to_rows(x_ref[0, :, qc]), heads_to_rows(x_ref[1, :, qc])
    return (q, do, *(got_ref[:, i, :, :, kc].reshape(n_keys, HD) for i in range(2)))


def stats_kernel(info_ref, x_ref, got_ref, out_ref):
    for g in range(2):
        q, do, k, v = row_parts(info_ref, x_ref, got_ref, g)
        e = jnp.exp2(dot(k, q, NT) * EXP2_SCALE)
        total = jnp.sum(e, axis=0, keepdims=True)
        inverse = jnp.where(total > 0, 1.0 / total, 0.0)
        delta = jnp.sum(e * inverse * dot(v, do, NT), axis=0, keepdims=True)
        rows = [a[:, h * BLK : (h + 1) * BLK] for a in (total, delta) for h in range(NH)]
        out_ref[g] = jnp.concatenate(rows, axis=0)


def row_kernel(info_ref, x_ref, got_ref, st_ref, dq_ref, down_ref):
    def lanes(a):
        return jnp.concatenate([a[h : h + 1] for h in range(NH)], axis=1)

    for g in range(2):
        q, do, k, v = row_parts(info_ref, x_ref, got_ref, g)
        inverse, mixed = 1.0 / st_ref[g, :NH, :], st_ref[g, NH:, :]
        p = jnp.exp2(dot(k, q, NT) * EXP2_SCALE) * lanes(inverse)
        pb = p.astype(BF16)
        ds = (p * (dot(v, do, NT) - lanes(mixed))).astype(BF16)
        dqt = dot(k, ds, TN) * SCALE
        dq_ref[:, g * NH * HD : (g + 1) * NH * HD] = jnp.concatenate(
            [dqt[:, h * HD : (h + 1) * HD].T for h in range(NH)], axis=1
        ).astype(BF16)
        kc = slice(g * HD, (g + 1) * HD)
        for i, grad in enumerate((dot(ds, q) * SCALE, dot(pb, do))):
            down_ref[:, i, :, :, kc] = grad.reshape(16, 2, 16, HD)


def place_kernel(info_ref, *refs):
    *part_refs, dq_ref, out_ref = refs
    width = part_refs[0].shape[1]

    @pl.when(info_ref[1] == 0)
    def _():
        for h in range(2):
            out_ref[:, h * width : (h + 1) * width] = part_refs[h][...]

    @pl.when(info_ref[1] != 0)
    def _():
        out_ref[...] = dq_ref[...]


def place(info, parts, dq):
    top = pl.BlockSpec((BLK, dq.shape[1]), lambda i, info: (0, 0))
    piece = pl.BlockSpec(parts[0].shape, lambda i, info: (0, 0))
    return pl.pallas_call(
        place_kernel,
        grid_spec=pltpu.PrefetchScalarGridSpec(
            num_scalar_prefetch=1, grid=(1,), in_specs=[piece] * 2 + [top], out_specs=top
        ),
        out_shape=stored(dq.shape, BF16),
        input_output_aliases={3: 0},
        compiler_params=params(12),
        name="place",
    )(info, *parts, dq)


def finish_kernel(info_ref, own_ref, winp_ref, winn_ref, got_ref, dk_ref, dv_ref):
    even = info_ref[1] % 2 == 0

    def total(first_ref, second_ref):
        for i, out_ref in enumerate((dk_ref, dv_ref)):
            for b, win_ref in enumerate((first_ref, second_ref)):
                for j in range(8):
                    rows = slice(b * BLK + j * 16, b * BLK + (j + 1) * 16)
                    pieces = got_ref[j, i, b].astype(F32) + got_ref[j + 8, i, b].astype(F32)
                    window = win_ref[i, j * 16 : (j + 1) * 16].astype(F32)
                    out_ref[rows, :] = (own_ref[i, rows, :] + pieces + window).astype(BF16)

    @pl.when(even)
    def _():
        total(winn_ref, winp_ref)

    @pl.when(jnp.logical_not(even))
    def _():
        total(winp_ref, winn_ref)


def send(block, pairs):
    return lax.ppermute(block, "ctx", pairs)


def add(a, *others):
    total = a.astype(F32)
    for o in others:
        total = total + o.astype(F32)
    return total.astype(BF16)


def merge_stats(mine, other):
    sums, deltas = zip(*((a[:, :NH], a[:, NH:]) for a in (mine, other)))
    total = sums[0] + sums[1]
    inverse = jnp.where(total > 0, 1.0 / total, 0.0)
    delta = (sums[0] * inverse) * deltas[0] + (sums[1] * inverse) * deltas[1]
    return jnp.concatenate([total, delta], axis=1)


def per_device(queries, keys, values, grad_slab, plan, random_blocks):
    n_seg, n_ctx = lax.axis_size("segment"), lax.axis_size("ctx")
    rank = lax.axis_index("ctx").astype(jnp.int32)
    queries, keys, values, grad = queries[0], keys[0], values[0], grad_slab[0]
    width, q_width = keys.shape[2], queries.shape[2]
    half = q_width // 2
    info = jnp.concatenate([plan, rank[None]])
    halves = [list(range(8)), list(range(8, 16))]
    slots = jnp.concatenate(
        [jnp.zeros((n_ctx, 1), jnp.int32), random_blocks.reshape(n_ctx, 6)], axis=1
    )
    side = rank // 8
    table = lax.dynamic_slice_in_dim(slots, side * 8, 8, 0).reshape(56)
    table = jnp.concatenate([table, side[None]])

    def exchange(x):
        return lax.all_to_all(x, "ctx", 0, 0, tiled=True)

    def exchange_half(x):
        return lax.all_to_all(x, "ctx", 0, 0, tiled=True, axis_index_groups=halves)

    both = ("segment", "ctx")

    def flat(s, r):
        return (s % n_seg) * n_ctx + r

    own, send1, edge, q0, q1, g0, g1 = pack(info, keys, values, queries, grad)
    q1 = send(q1, [(0, 8)])
    g0 = lax.ppermute(g0, both, [(flat(s + 1, 0), flat(s, 0)) for s in range(n_seg)])
    g1 = lax.ppermute(g1, both, [(flat(s + 1, 0), flat(s, 8)) for s in range(n_seg)])
    got1 = exchange(send1)
    x = jnp.stack([jnp.where(rank == 0, q0, jnp.zeros((), BF16)) + q1, g0 + g1])
    swap = [(r, r ^ 1) for r in range(n_ctx)]
    ring = [(r, (r - 1 if r % 2 == 0 else r + 1) % n_ctx) for r in range(n_ctx)]
    partner, neighbour = send(own, swap), send(edge, ring)
    x = x + sum(send(x, [(r, r + 2 * y) for r in (0, 8)]) for y in (1, 2, 3))
    x, got1, grad, partner, neighbour = lax.optimization_barrier(
        (x, got1, grad, partner, neighbour)
    )
    upstream = lax.ppermute(grad, "segment", [((s + 1) % n_seg, s) for s in range(n_seg)])
    (send2,) = on_chip(select_kernel, "select", [stored((8, 2, 7, 16, width), BF16)], table, got1)
    got2 = exchange_half(send2)
    x = x + send(x, [(r, r + 1) for r in range(0, n_ctx, 2)])
    (stats,) = on_chip(stats_kernel, "row_stats", [stored((2, 8, BLK), F32)], info, x, got1)
    stats = merge_stats(stats, send(stats, swap))
    others = [
        send(stats, [(r, (r // 8) * 8 + (r + 2 * y) % 8) for r in range(n_ctx)]) for y in (1, 2, 3)
    ]
    got2, stats, *others = lax.optimization_barrier((got2, stats, *others))
    dq, down, winp, winn, send3 = attend(
        info, queries, upstream, own, partner, neighbour, got2
    )
    got3 = exchange_half(send3)
    stats, *others = lax.optimization_barrier((stats, *others, send3))[:4]
    stats = merge_stats(merge_stats(stats, others[1]), merge_stats(others[0], others[2]))
    part, row = on_chip(
        row_kernel,
        "row_grads",
        [stored((BLK, half), BF16), stored((16, 2, 2, 16, 2 * HD), F32)],
        info, x, got1, stats,
    )
    winp, winn = send(winp, swap), send(winn, ring)
    part = add(part, send(part, [(r + 1, r) for r in range(0, n_ctx, 2)]))
    near = [send(part, [(2 * y, 0), (8 + 2 * y, 1)]) for y in (1, 2, 3)]
    far = send(part, [(8, 1)])
    got3, winp, part, far, *near = lax.optimization_barrier((got3, winp, part, far, *near))

    (send4,) = on_chip(
        combine_kernel,
        "combine",
        [stored((16, 2, 2, 16, width), BF16)],
        table, got3, row,
        scratch=[pltpu.VMEM((16, 2, 2, 16, width), F32)],
    )
    got4 = exchange(send4)
    part = after(add(jnp.where(rank == 1, far, part), *near), send4)
    dq = place(info, [part, send(part, [(1, 0)])], dq)
    got4, dq = lax.optimization_barrier((got4, dq))
    dk, dv = on_chip(
        finish_kernel,
        "finish",
        [shape((2 * BLK, width), BF16)] * 2,
        info, down, winp, winn, got4,
    )
    return dq[None], dk[None], dv[None]


def solution(mesh):
    return jax.shard_map(
        per_device,
        mesh=mesh,
        in_specs=(
            P("segment", None, "ctx", None),
            P("segment", None, "ctx", None),
            P("segment", None, "ctx", None),
            P("segment", "ctx", None),
            P("segment"),
            P(),
        ),
        out_specs=(P("segment", "ctx", None), P("segment", "ctx", None), P("segment", "ctx", None)),
        check_vma=False,
    )
```

```python
import functools
import math

import jax
import jax.numpy as jnp
from jax import lax
from jax.experimental import pallas as pl
from jax.experimental.pallas import tpu as pltpu
from jax.sharding import PartitionSpec as P

HD = 128
BLK = 128
NH = 4
SCALE = HD**-0.5
EXP2_SCALE = SCALE * math.log2(math.e)
F32 = jnp.float32
BF16 = jnp.bfloat16
NT = (((1,), (1,)), ((), ()))
TN = (((0,), (0,)), ((), ()))
MIB = 2**20


def dot(a, b, dims=(((1,), (0,)), ((), ()))):
    return lax.dot_general(a, b, dims, preferred_element_type=F32)


def params(mib=8):
    return pltpu.CompilerParams(vmem_limit_bytes=mib * MIB)


def on_chip(kernel, name, out_shape, *operands, scratch=(), mib=8):
    vmem = pl.BlockSpec(memory_space=pltpu.VMEM)
    return pl.pallas_call(
        kernel,
        in_specs=[pl.BlockSpec(memory_space=pltpu.SMEM)] + [vmem] * (len(operands) - 1),
        out_specs=[vmem] * len(out_shape),
        out_shape=out_shape,
        scratch_shapes=list(scratch),
        compiler_params=params(mib),
        name=name,
    )(*operands)


def shape(dims, dtype):
    return jax.ShapeDtypeStruct(dims, dtype)


def stored(dims, dtype):
    return pltpu.HBM(dims, dtype)


def after(x, *others):
    return lax.optimization_barrier((x, *others))[0]


def pack_kernel(
    info_ref, k_ref, v_ref, q_ref, g_ref,
    kv_ref, send_ref, edge_ref, q0_ref, q1_ref, g0_ref, g1_ref,
):
    edge = pl.ds(pl.multiple_of(info_ref[1] % 2 * BLK, BLK), BLK)
    for i, ref in enumerate((k_ref, v_ref)):
        kv_ref[i] = ref[0]
        edge_ref[i] = ref[0, edge, :]
        for b in range(2):
            for j in range(8):
                piece = ref[0, b * BLK + j * 16 : b * BLK + (j + 1) * 16, :]
                send_ref[j, i, b] = piece
                send_ref[j + 8, i, b] = piece
    half = q0_ref.shape[1]
    q0_ref[...] = q_ref[0, :, :half]
    q1_ref[...] = q_ref[0, :, half:]
    g0_ref[...] = g_ref[:, :half]
    g1_ref[...] = g_ref[:, half:]


def pack(info, keys, values, queries, grad):
    width, q_width = keys.shape[2], queries.shape[2]
    spec = pl.BlockSpec((1, 2 * BLK, width), lambda i, info: (info[0], 0, 0))
    half = pl.BlockSpec((BLK, q_width // 2), lambda i, info: (0, 0))
    inputs = [pltpu.with_memory_space_constraint(a, pltpu.HBM) for a in (keys, values, queries, grad)]
    return pl.pallas_call(
        pack_kernel,
        grid_spec=pltpu.PrefetchScalarGridSpec(
            num_scalar_prefetch=1,
            grid=(1,),
            in_specs=[
                spec,
                spec,
                pl.BlockSpec((1, BLK, q_width), lambda i, info: (info[0], 0, 0)),
                pl.BlockSpec((BLK, q_width), lambda i, info: (0, 0)),
            ],
            out_specs=[
                pl.BlockSpec((2, 2 * BLK, width), lambda i, info: (0, 0, 0)),
                pl.BlockSpec((16, 2, 2, 16, width), lambda i, info: (0, 0, 0, 0, 0)),
                pl.BlockSpec((2, BLK, width), lambda i, info: (0, 0, 0)),
                *[half] * 4,
            ],
        ),
        out_shape=[
            stored((2, 2 * BLK, width), BF16),
            stored((16, 2, 2, 16, width), BF16),
            stored((2, BLK, width), BF16),
            *[stored((BLK, q_width // 2), BF16)] * 4,
        ],
        compiler_params=params(16),
        name="pack",
    )(info, *inputs)


def select_kernel(table_ref, got_ref, send_ref):
    for d in range(8):
        for s in range(7):
            block = table_ref[d * 7 + s]
            owner, which = block // 2, block % 2
            for i in range(2):
                send_ref[d, i, s] = got_ref[owner, i, which]


def combine_kernel(table_ref, got_ref, row_ref, send_ref, acc_ref):
    acc_ref[...] = jnp.zeros_like(acc_ref)
    acc_ref[:, :, :, :, columns(table_ref[56], 2 * HD)] = row_ref[...]
    for d in range(8):
        for s in range(7):
            block = table_ref[d * 7 + s]
            owner, which = block // 2, block % 2
            for i in range(2):
                acc_ref[owner, i, which] += got_ref[d, i, s].astype(F32)
    send_ref[...] = acc_ref[...].astype(BF16)


def heads_to_rows(cols):
    return jnp.concatenate([cols[:, h * HD : (h + 1) * HD] for h in range(NH)], axis=0)


def columns(g, width):
    return pl.ds(pl.multiple_of(g * width, width), width)


def attend_kernel(
    info_ref, q_ref, do_ref, own_ref, part_ref, nb_ref, rv_ref,
    dq_ref, down_ref, winp_ref, winn_ref, send_ref, wk_ref, zero_ref,
):
    rank = info_ref[1]
    even = rank % 2 == 0

    @pl.when(even)
    def _():
        wk_ref[0] = nb_ref[...]
        wk_ref[1] = part_ref[:, :BLK, :]

    @pl.when(jnp.logical_not(even))
    def _():
        wk_ref[0] = part_ref[:, BLK:, :]
        wk_ref[1] = nb_ref[...]

    def operands(n):
        rows = slice(n * BLK, (n + 1) * BLK)
        q, do = heads_to_rows(q_ref[0, rows, :]), heads_to_rows(do_ref[rows, :])

        def blocks(i):
            parts = [own_ref[i], wk_ref[n, i], rv_ref[:, i, 0].reshape(BLK, HD)]
            parts += [rv_ref[:, i, 1 + 3 * n + j].reshape(BLK, HD) for j in range(3)]
            return jnp.concatenate(parts, axis=0)

        return q, do, blocks(0), blocks(1)

    def exp_scores(n, q, do, k, v):
        e = jnp.exp2(dot(k, q, NT) * EXP2_SCALE)
        if n == 1:
            twice = jnp.logical_or(rank == 0, rank == 15)
            keep = jnp.where(twice, 0.0, 1.0).astype(F32)
            e = jnp.concatenate([e[: 3 * BLK], e[3 * BLK : 4 * BLK] * keep, e[4 * BLK :]], axis=0)
        return e

    def weights(e, q, do, k, v):
        p = e * (1.0 / jnp.sum(e, axis=0, keepdims=True))
        dp = dot(v, do, NT)
        delta = jnp.sum(p * dp, axis=0, keepdims=True)
        return p.astype(BF16), (p * (dp - delta)).astype(BF16)

    def grads(n, pb, ds, q, do, k, v):
        dqt = dot(k, ds, TN) * SCALE
        dq_ref[n * BLK : (n + 1) * BLK, :] = jnp.concatenate(
            [dqt[:, h * HD : (h + 1) * HD].T for h in range(NH)], axis=1
        ).astype(BF16)
        return dot(ds, q) * SCALE, dot(pb, do)

    def emit(n, grads):
        for i, grad in enumerate(grads):
            if n == 0:
                down_ref[i] = grad[: 2 * BLK]
                zero_ref[i] = grad[3 * BLK : 4 * BLK]
            else:
                down_ref[i] += grad[: 2 * BLK]
                total = zero_ref[i] + grad[3 * BLK : 4 * BLK]
                send_ref[:, i, 0] = total.astype(BF16).reshape(8, 16, HD)
            wk_ref[n, i] = grad[2 * BLK : 3 * BLK].astype(BF16)
            for j in range(3):
                got = grad[(4 + j) * BLK : (5 + j) * BLK].astype(BF16)
                send_ref[:, i, 1 + 3 * n + j] = got.reshape(8, 16, HD)

    given = [operands(n) for n in range(2)]
    scores = [exp_scores(n, *given[n]) for n in range(2)]
    shares = [weights(scores[n], *given[n]) for n in range(2)]
    first, second = (grads(n, *shares[n], *given[n]) for n in range(2))
    emit(0, [jnp.where(rank != 0, term, 0.0) for term in first])
    emit(1, second)

    @pl.when(even)
    def _():
        winn_ref[...] = wk_ref[0]
        winp_ref[...] = wk_ref[1]

    @pl.when(jnp.logical_not(even))
    def _():
        winp_ref[...] = wk_ref[0]
        winn_ref[...] = wk_ref[1]


def attend(info, queries, upstream, own, partner, neighbour, got):
    q_width, width = queries.shape[2], own.shape[2]
    kv_spec = pl.BlockSpec((2, 2 * BLK, HD), lambda g, info: (0, 0, g))
    win_spec = pl.BlockSpec((2, BLK, HD), lambda g, info: (0, 0, g))
    piece_spec = pl.BlockSpec((8, 2, 7, 16, HD), lambda g, info: (0, 0, 0, 0, g))
    row_spec = pl.BlockSpec((2 * BLK, NH * HD), lambda g, info: (0, g))
    return pl.pallas_call(
        attend_kernel,
        grid_spec=pltpu.PrefetchScalarGridSpec(
            num_scalar_prefetch=1,
            grid=(width // HD,),
            in_specs=[
                pl.BlockSpec((1, 2 * BLK, NH * HD), lambda g, info: (info[0], 0, g)),
                row_spec, kv_spec, kv_spec, win_spec, piece_spec,
            ],
            out_specs=[row_spec, kv_spec, win_spec, win_spec, piece_spec],
            scratch_shapes=[pltpu.VMEM((2, 2, BLK, HD), BF16), pltpu.VMEM((2, BLK, HD), F32)],
        ),
        out_shape=[
            stored((2 * BLK, q_width), BF16),
            stored((2, 2 * BLK, width), F32),
            stored((2, BLK, width), BF16),
            stored((2, BLK, width), BF16),
            stored((8, 2, 7, 16, width), BF16),
        ],
        compiler_params=params(28),
        cost_estimate=pl.CostEstimate(
            flops=10 * q_width * 14 * BLK * BLK, transcendentals=q_width * 14 * BLK, bytes_accessed=10 * MIB
        ),
        name="attend",
    )(
        info,
        *(
            pltpu.with_memory_space_constraint(a, pltpu.HBM)
            for a in (queries, upstream, own, partner, neighbour)
        ),
        got,
    )


def row_parts(info_ref, x_ref, got_ref, g):
    kc = columns(2 * (info_ref[1] // 8) + g, HD)
    qc = slice(g * NH * HD, (g + 1) * NH * HD)
    n_keys = got_ref.shape[0] * 2 * 16
    q, do = heads_to_rows(x_ref[0, :, qc]), heads_to_rows(x_ref[1, :, qc])
    return (q, do, *(got_ref[:, i, :, :, kc].reshape(n_keys, HD) for i in range(2)))


def stats_kernel(info_ref, x_ref, got_ref, out_ref):
    for g in range(2):
        q, do, k, v = row_parts(info_ref, x_ref, got_ref, g)
        e = jnp.exp2(dot(k, q, NT) * EXP2_SCALE)
        total = jnp.sum(e, axis=0, keepdims=True)
        inverse = jnp.where(total > 0, 1.0 / total, 0.0)
        delta = jnp.sum(e * inverse * dot(v, do, NT), axis=0, keepdims=True)
        rows = [a[:, h * BLK : (h + 1) * BLK] for a in (total, delta) for h in range(NH)]
        out_ref[g] = jnp.concatenate(rows, axis=0)


def row_kernel(info_ref, x_ref, got_ref, st_ref, dq_ref, down_ref):
    def lanes(a):
        return jnp.concatenate([a[h : h + 1] for h in range(NH)], axis=1)

    for g in range(2):
        q, do, k, v = row_parts(info_ref, x_ref, got_ref, g)
        inverse, mixed = 1.0 / st_ref[g, :NH, :], st_ref[g, NH:, :]
        p = jnp.exp2(dot(k, q, NT) * EXP2_SCALE) * lanes(inverse)
        pb = p.astype(BF16)
        ds = (p * (dot(v, do, NT) - lanes(mixed))).astype(BF16)
        dqt = dot(k, ds, TN) * SCALE
        dq_ref[:, g * NH * HD : (g + 1) * NH * HD] = jnp.concatenate(
            [dqt[:, h * HD : (h + 1) * HD].T for h in range(NH)], axis=1
        ).astype(BF16)
        kc = slice(g * HD, (g + 1) * HD)
        for i, grad in enumerate((dot(ds, q) * SCALE, dot(pb, do))):
            down_ref[:, i, :, :, kc] = grad.reshape(16, 2, 16, HD)


def place_kernel(info_ref, *refs):
    *part_refs, dq_ref, out_ref = refs
    width = part_refs[0].shape[1]

    @pl.when(info_ref[1] == 0)
    def _():
        for h in range(2):
            out_ref[:, h * width : (h + 1) * width] = part_refs[h][...]

    @pl.when(info_ref[1] != 0)
    def _():
        out_ref[...] = dq_ref[...]


def place(info, parts, dq):
    top = pl.BlockSpec((BLK, dq.shape[1]), lambda i, info: (0, 0))
    piece = pl.BlockSpec(parts[0].shape, lambda i, info: (0, 0))
    return pl.pallas_call(
        place_kernel,
        grid_spec=pltpu.PrefetchScalarGridSpec(
            num_scalar_prefetch=1, grid=(1,), in_specs=[piece] * 2 + [top], out_specs=top
        ),
        out_shape=stored(dq.shape, BF16),
        input_output_aliases={3: 0},
        compiler_params=params(12),
        name="place",
    )(info, *parts, dq)


def finish_kernel(info_ref, own_ref, winp_ref, winn_ref, got_ref, dk_ref, dv_ref):
    even = info_ref[1] % 2 == 0

    def total(first_ref, second_ref):
        for i, out_ref in enumerate((dk_ref, dv_ref)):
            for b, win_ref in enumerate((first_ref, second_ref)):
                for j in range(8):
                    rows = slice(b * BLK + j * 16, b * BLK + (j + 1) * 16)
                    pieces = got_ref[j, i, b].astype(F32) + got_ref[j + 8, i, b].astype(F32)
                    window = win_ref[i, j * 16 : (j + 1) * 16].astype(F32)
                    out_ref[rows, :] = (own_ref[i, rows, :] + pieces + window).astype(BF16)

    @pl.when(even)
    def _():
        total(winn_ref, winp_ref)

    @pl.when(jnp.logical_not(even))
    def _():
        total(winp_ref, winn_ref)


def send(block, pairs):
    return lax.ppermute(block, "ctx", pairs)


def add(a, *others):
    total = a.astype(F32)
    for o in others:
        total = total + o.astype(F32)
    return total.astype(BF16)


def merge_stats(mine, other):
    sums, deltas = zip(*((a[:, :NH], a[:, NH:]) for a in (mine, other)))
    total = sums[0] + sums[1]
    inverse = jnp.where(total > 0, 1.0 / total, 0.0)
    delta = (sums[0] * inverse) * deltas[0] + (sums[1] * inverse) * deltas[1]
    return jnp.concatenate([total, delta], axis=1)


def per_device(queries, keys, values, grad_slab, plan, random_blocks):
    n_seg, n_ctx = lax.axis_size("segment"), lax.axis_size("ctx")
    rank = lax.axis_index("ctx").astype(jnp.int32)
    queries, keys, values, grad = queries[0], keys[0], values[0], grad_slab[0]
    width, q_width = keys.shape[2], queries.shape[2]
    half = q_width // 2
    info = jnp.concatenate([plan, rank[None]])
    halves = [list(range(8)), list(range(8, 16))]
    slots = jnp.concatenate(
        [jnp.zeros((n_ctx, 1), jnp.int32), random_blocks.reshape(n_ctx, 6)], axis=1
    )
    side = rank // 8
    table = lax.dynamic_slice_in_dim(slots, side * 8, 8, 0).reshape(56)
    table = jnp.concatenate([table, side[None]])

    def exchange(x):
        return lax.all_to_all(x, "ctx", 0, 0, tiled=True)

    def exchange_half(x):
        return lax.all_to_all(x, "ctx", 0, 0, tiled=True, axis_index_groups=halves)

    both = ("segment", "ctx")

    def flat(s, r):
        return (s % n_seg) * n_ctx + r

    own, send1, edge, q0, q1, g0, g1 = pack(info, keys, values, queries, grad)
    q1 = send(q1, [(0, 8)])
    g0 = lax.ppermute(g0, both, [(flat(s + 1, 0), flat(s, 0)) for s in range(n_seg)])
    g1 = lax.ppermute(g1, both, [(flat(s + 1, 0), flat(s, 8)) for s in range(n_seg)])
    got1 = exchange(send1)
    x = jnp.stack([jnp.where(rank == 0, q0, jnp.zeros((), BF16)) + q1, g0 + g1])
    swap = [(r, r ^ 1) for r in range(n_ctx)]
    ring = [(r, (r - 1 if r % 2 == 0 else r + 1) % n_ctx) for r in range(n_ctx)]
    partner, neighbour = send(own, swap), send(edge, ring)
    spread = [send(x, [(r, r + 2 * y) for r in (0, 8)]) for y in (1, 2, 3)]
    (send2,) = on_chip(select_kernel, "select", [stored((8, 2, 7, 16, width), BF16)], table, got1)
    x = after(x, send2) + sum(spread)
    x, send2, got1, grad, partner, neighbour = lax.optimization_barrier(
        (x, send2, got1, grad, partner, neighbour)
    )
    upstream = lax.ppermute(grad, "segment", [((s + 1) % n_seg, s) for s in range(n_seg)])
    got2 = exchange_half(send2)
    x = x + send(x, [(r, r + 1) for r in range(0, n_ctx, 2)])
    (stats,) = on_chip(stats_kernel, "row_stats", [stored((2, 8, BLK), F32)], info, x, got1)
    stats = merge_stats(stats, send(stats, swap))
    others = [
        send(stats, [(r, (r // 8) * 8 + (r + 2 * y) % 8) for r in range(n_ctx)]) for y in (1, 2, 3)
    ]
    got2, stats, *others = lax.optimization_barrier((got2, stats, *others))
    dq, down, winp, winn, send3 = attend(
        info, queries, upstream, own, partner, neighbour, got2
    )
    got3 = exchange_half(send3)
    stats, *others = lax.optimization_barrier((stats, *others, send3))[:4]
    stats = merge_stats(merge_stats(stats, others[1]), merge_stats(others[0], others[2]))
    part, row = on_chip(
        row_kernel,
        "row_grads",
        [stored((BLK, half), BF16), stored((16, 2, 2, 16, 2 * HD), F32)],
        info, x, got1, stats,
    )
    winp, winn = send(winp, swap), send(winn, ring)
    part = add(part, send(part, [(r + 1, r) for r in range(0, n_ctx, 2)]))
    near = [send(part, [(2 * y, 0), (8 + 2 * y, 1)]) for y in (1, 2, 3)]
    far = send(part, [(8, 1)])
    got3, winp, part, far, *near = lax.optimization_barrier((got3, winp, part, far, *near))

    (send4,) = on_chip(
        combine_kernel,
        "combine",
        [stored((16, 2, 2, 16, width), BF16)],
        table, got3, row,
        scratch=[pltpu.VMEM((16, 2, 2, 16, width), F32)],
    )
    got4 = exchange(send4)
    part = after(add(jnp.where(rank == 1, far, part), *near), send4)
    dq = place(info, [part, send(part, [(1, 0)])], dq)
    got4, dq = lax.optimization_barrier((got4, dq))
    dk, dv = on_chip(
        finish_kernel,
        "finish",
        [shape((2 * BLK, width), BF16)] * 2,
        info, down, winp, winn, got4,
    )
    return dq[None], dk[None], dv[None]


def solution(mesh):
    return jax.shard_map(
        per_device,
        mesh=mesh,
        in_specs=(
            P("segment", None, "ctx", None),
            P("segment", None, "ctx", None),
            P("segment", None, "ctx", None),
            P("segment", "ctx", None),
            P("segment"),
            P(),
        ),
        out_specs=(P("segment", "ctx", None), P("segment", "ctx", None), P("segment", "ctx", None)),
        check_vma=False,
    )
```

```python
import functools
import math

import jax
import jax.numpy as jnp
from jax import lax
from jax.experimental import pallas as pl
from jax.experimental.pallas import tpu as pltpu
from jax.sharding import PartitionSpec as P

HD = 128
BLK = 128
NH = 4
SCALE = HD**-0.5
EXP2_SCALE = SCALE * math.log2(math.e)
F32 = jnp.float32
BF16 = jnp.bfloat16
NT = (((1,), (1,)), ((), ()))
TN = (((0,), (0,)), ((), ()))
MIB = 2**20


def dot(a, b, dims=(((1,), (0,)), ((), ()))):
    return lax.dot_general(a, b, dims, preferred_element_type=F32)


def params(mib=8):
    return pltpu.CompilerParams(vmem_limit_bytes=mib * MIB)


def on_chip(kernel, name, out_shape, *operands, scratch=(), mib=8):
    vmem = pl.BlockSpec(memory_space=pltpu.VMEM)
    return pl.pallas_call(
        kernel,
        in_specs=[pl.BlockSpec(memory_space=pltpu.SMEM)] + [vmem] * (len(operands) - 1),
        out_specs=[vmem] * len(out_shape),
        out_shape=out_shape,
        scratch_shapes=list(scratch),
        compiler_params=params(mib),
        name=name,
    )(*operands)


def shape(dims, dtype):
    return jax.ShapeDtypeStruct(dims, dtype)


def stored(dims, dtype):
    return pltpu.HBM(dims, dtype)


def after(x, *others):
    return lax.optimization_barrier((x, *others))[0]


def pack_kernel(
    info_ref, k_ref, v_ref, q_ref, g_ref,
    kv_ref, send_ref, edge_ref, q0_ref, q1_ref, g0_ref, g1_ref,
):
    edge = pl.ds(pl.multiple_of(info_ref[1] % 2 * BLK, BLK), BLK)
    for i, ref in enumerate((k_ref, v_ref)):
        kv_ref[i] = ref[0]
        edge_ref[i] = ref[0, edge, :]
        for b in range(2):
            for j in range(8):
                piece = ref[0, b * BLK + j * 16 : b * BLK + (j + 1) * 16, :]
                send_ref[j, i, b] = piece
                send_ref[j + 8, i, b] = piece
    half = q0_ref.shape[1]
    q0_ref[...] = q_ref[0, :, :half]
    q1_ref[...] = q_ref[0, :, half:]
    g0_ref[...] = g_ref[:, :half]
    g1_ref[...] = g_ref[:, half:]


def pack(info, keys, values, queries, grad):
    width, q_width = keys.shape[2], queries.shape[2]
    spec = pl.BlockSpec((1, 2 * BLK, width), lambda i, info: (info[0], 0, 0))
    half = pl.BlockSpec((BLK, q_width // 2), lambda i, info: (0, 0))
    inputs = [pltpu.with_memory_space_constraint(a, pltpu.HBM) for a in (keys, values, queries, grad)]
    return pl.pallas_call(
        pack_kernel,
        grid_spec=pltpu.PrefetchScalarGridSpec(
            num_scalar_prefetch=1,
            grid=(1,),
            in_specs=[
                spec,
                spec,
                pl.BlockSpec((1, BLK, q_width), lambda i, info: (info[0], 0, 0)),
                pl.BlockSpec((BLK, q_width), lambda i, info: (0, 0)),
            ],
            out_specs=[
                pl.BlockSpec((2, 2 * BLK, width), lambda i, info: (0, 0, 0)),
                pl.BlockSpec((16, 2, 2, 16, width), lambda i, info: (0, 0, 0, 0, 0)),
                pl.BlockSpec((2, BLK, width), lambda i, info: (0, 0, 0)),
                *[half] * 4,
            ],
        ),
        out_shape=[
            stored((2, 2 * BLK, width), BF16),
            stored((16, 2, 2, 16, width), BF16),
            stored((2, BLK, width), BF16),
            *[stored((BLK, q_width // 2), BF16)] * 4,
        ],
        compiler_params=params(16),
        name="pack",
    )(info, *inputs)


def select_kernel(table_ref, got_ref, send_ref):
    for d in range(8):
        for s in range(7):
            block = table_ref[d * 7 + s]
            owner, which = block // 2, block % 2
            for i in range(2):
                send_ref[d, i, s] = got_ref[owner, i, which]


def combine_kernel(table_ref, got_ref, row_ref, send_ref, acc_ref):
    acc_ref[...] = jnp.zeros_like(acc_ref)
    acc_ref[:, :, :, :, columns(table_ref[56], 2 * HD)] = row_ref[...]
    for d in range(8):
        for s in range(7):
            block = table_ref[d * 7 + s]
            owner, which = block // 2, block % 2
            for i in range(2):
                acc_ref[owner, i, which] += got_ref[d, i, s].astype(F32)
    send_ref[...] = acc_ref[...].astype(BF16)


def heads_to_rows(cols):
    return jnp.concatenate([cols[:, h * HD : (h + 1) * HD] for h in range(NH)], axis=0)


def columns(g, width):
    return pl.ds(pl.multiple_of(g * width, width), width)


def attend_kernel(
    info_ref, q_ref, do_ref, own_ref, part_ref, nb_ref, rv_ref,
    dq_ref, down_ref, winp_ref, winn_ref, send_ref, wk_ref, zero_ref,
):
    rank = info_ref[1]
    even = rank % 2 == 0

    @pl.when(even)
    def _():
        wk_ref[0] = nb_ref[...]
        wk_ref[1] = part_ref[:, :BLK, :]

    @pl.when(jnp.logical_not(even))
    def _():
        wk_ref[0] = part_ref[:, BLK:, :]
        wk_ref[1] = nb_ref[...]

    def operands(n):
        rows = slice(n * BLK, (n + 1) * BLK)
        q, do = heads_to_rows(q_ref[0, rows, :]), heads_to_rows(do_ref[rows, :])

        def blocks(i):
            parts = [own_ref[i], wk_ref[n, i], rv_ref[:, i, 0].reshape(BLK, HD)]
            parts += [rv_ref[:, i, 1 + 3 * n + j].reshape(BLK, HD) for j in range(3)]
            return jnp.concatenate(parts, axis=0)

        return q, do, blocks(0), blocks(1)

    def exp_scores(n, q, do, k, v):
        e = jnp.exp2(dot(k, q, NT) * EXP2_SCALE)
        if n == 1:
            twice = jnp.logical_or(rank == 0, rank == 15)
            keep = jnp.where(twice, 0.0, 1.0).astype(F32)
            e = jnp.concatenate([e[: 3 * BLK], e[3 * BLK : 4 * BLK] * keep, e[4 * BLK :]], axis=0)
        return e

    def weights(e, q, do, k, v):
        p = e * (1.0 / jnp.sum(e, axis=0, keepdims=True))
        dp = dot(v, do, NT)
        delta = jnp.sum(p * dp, axis=0, keepdims=True)
        return p.astype(BF16), (p * (dp - delta)).astype(BF16)

    def grads(n, pb, ds, q, do, k, v):
        dqt = dot(k, ds, TN) * SCALE
        dq_ref[n * BLK : (n + 1) * BLK, :] = jnp.concatenate(
            [dqt[:, h * HD : (h + 1) * HD].T for h in range(NH)], axis=1
        ).astype(BF16)
        return dot(ds, q) * SCALE, dot(pb, do)

    def emit(n, grads):
        for i, grad in enumerate(grads):
            if n == 0:
                down_ref[i] = grad[: 2 * BLK]
                zero_ref[i] = grad[3 * BLK : 4 * BLK]
            else:
                down_ref[i] += grad[: 2 * BLK]
                total = zero_ref[i] + grad[3 * BLK : 4 * BLK]
                send_ref[:, i, 0] = total.astype(BF16).reshape(8, 16, HD)
            wk_ref[n, i] = grad[2 * BLK : 3 * BLK].astype(BF16)
            for j in range(3):
                got = grad[(4 + j) * BLK : (5 + j) * BLK].astype(BF16)
                send_ref[:, i, 1 + 3 * n + j] = got.reshape(8, 16, HD)

    given = [operands(n) for n in range(2)]
    scores = [exp_scores(n, *given[n]) for n in range(2)]
    shares = [weights(scores[n], *given[n]) for n in range(2)]
    first, second = (grads(n, *shares[n], *given[n]) for n in range(2))
    emit(0, [jnp.where(rank != 0, term, 0.0) for term in first])
    emit(1, second)

    @pl.when(even)
    def _():
        winn_ref[...] = wk_ref[0]
        winp_ref[...] = wk_ref[1]

    @pl.when(jnp.logical_not(even))
    def _():
        winp_ref[...] = wk_ref[0]
        winn_ref[...] = wk_ref[1]


def attend(info, queries, upstream, own, partner, neighbour, got):
    q_width, width = queries.shape[2], own.shape[2]
    kv_spec = pl.BlockSpec((2, 2 * BLK, HD), lambda g, info: (0, 0, g))
    win_spec = pl.BlockSpec((2, BLK, HD), lambda g, info: (0, 0, g))
    piece_spec = pl.BlockSpec((8, 2, 7, 16, HD), lambda g, info: (0, 0, 0, 0, g))
    row_spec = pl.BlockSpec((2 * BLK, NH * HD), lambda g, info: (0, g))
    return pl.pallas_call(
        attend_kernel,
        grid_spec=pltpu.PrefetchScalarGridSpec(
            num_scalar_prefetch=1,
            grid=(width // HD,),
            in_specs=[
                pl.BlockSpec((1, 2 * BLK, NH * HD), lambda g, info: (info[0], 0, g)),
                row_spec, kv_spec, kv_spec, win_spec, piece_spec,
            ],
            out_specs=[row_spec, kv_spec, win_spec, win_spec, piece_spec],
            scratch_shapes=[pltpu.VMEM((2, 2, BLK, HD), BF16), pltpu.VMEM((2, BLK, HD), F32)],
        ),
        out_shape=[
            stored((2 * BLK, q_width), BF16),
            stored((2, 2 * BLK, width), F32),
            stored((2, BLK, width), BF16),
            stored((2, BLK, width), BF16),
            stored((8, 2, 7, 16, width), BF16),
        ],
        compiler_params=params(28),
        cost_estimate=pl.CostEstimate(
            flops=10 * q_width * 14 * BLK * BLK, transcendentals=q_width * 14 * BLK, bytes_accessed=10 * MIB
        ),
        name="attend",
    )(
        info,
        *(
            pltpu.with_memory_space_constraint(a, pltpu.HBM)
            for a in (queries, upstream, own, partner, neighbour)
        ),
        got,
    )


def row_parts(info_ref, x_ref, got_ref, g):
    kc = columns(2 * (info_ref[1] // 8) + g, HD)
    qc = slice(g * NH * HD, (g + 1) * NH * HD)
    n_keys = got_ref.shape[0] * 2 * 16
    q, do = heads_to_rows(x_ref[0, :, qc]), heads_to_rows(x_ref[1, :, qc])
    return (q, do, *(got_ref[:, i, :, :, kc].reshape(n_keys, HD) for i in range(2)))


def stats_kernel(info_ref, x_ref, got_ref, out_ref):
    for g in range(2):
        q, do, k, v = row_parts(info_ref, x_ref, got_ref, g)
        e = jnp.exp2(dot(k, q, NT) * EXP2_SCALE)
        total = jnp.sum(e, axis=0, keepdims=True)
        inverse = jnp.where(total > 0, 1.0 / total, 0.0)
        delta = jnp.sum(e * inverse * dot(v, do, NT), axis=0, keepdims=True)
        rows = [a[:, h * BLK : (h + 1) * BLK] for a in (total, delta) for h in range(NH)]
        out_ref[g] = jnp.concatenate(rows, axis=0)


def row_kernel(info_ref, x_ref, got_ref, st_ref, dq_ref, down_ref):
    def lanes(a):
        return jnp.concatenate([a[h : h + 1] for h in range(NH)], axis=1)

    for g in range(2):
        q, do, k, v = row_parts(info_ref, x_ref, got_ref, g)
        inverse, mixed = 1.0 / st_ref[g, :NH, :], st_ref[g, NH:, :]
        p = jnp.exp2(dot(k, q, NT) * EXP2_SCALE) * lanes(inverse)
        pb = p.astype(BF16)
        ds = (p * (dot(v, do, NT) - lanes(mixed))).astype(BF16)
        dqt = dot(k, ds, TN) * SCALE
        dq_ref[:, g * NH * HD : (g + 1) * NH * HD] = jnp.concatenate(
            [dqt[:, h * HD : (h + 1) * HD].T for h in range(NH)], axis=1
        ).astype(BF16)
        kc = slice(g * HD, (g + 1) * HD)
        for i, grad in enumerate((dot(ds, q) * SCALE, dot(pb, do))):
            down_ref[:, i, :, :, kc] = grad.reshape(16, 2, 16, HD)


def place_kernel(info_ref, *refs):
    *part_refs, dq_ref, out_ref = refs
    width = part_refs[0].shape[1]

    @pl.when(info_ref[1] == 0)
    def _():
        for h in range(2):
            out_ref[:, h * width : (h + 1) * width] = part_refs[h][...]

    @pl.when(info_ref[1] != 0)
    def _():
        out_ref[...] = dq_ref[...]


def place(info, parts, dq):
    top = pl.BlockSpec((BLK, dq.shape[1]), lambda i, info: (0, 0))
    piece = pl.BlockSpec(parts[0].shape, lambda i, info: (0, 0))
    return pl.pallas_call(
        place_kernel,
        grid_spec=pltpu.PrefetchScalarGridSpec(
            num_scalar_prefetch=1, grid=(1,), in_specs=[piece] * 2 + [top], out_specs=top
        ),
        out_shape=stored(dq.shape, BF16),
        input_output_aliases={3: 0},
        compiler_params=params(12),
        name="place",
    )(info, *parts, dq)


def finish_kernel(info_ref, own_ref, winp_ref, winn_ref, got_ref, dk_ref, dv_ref):
    even = info_ref[1] % 2 == 0

    def total(first_ref, second_ref):
        for i, out_ref in enumerate((dk_ref, dv_ref)):
            for b, win_ref in enumerate((first_ref, second_ref)):
                for j in range(8):
                    rows = slice(b * BLK + j * 16, b * BLK + (j + 1) * 16)
                    pieces = got_ref[j, i, b].astype(F32) + got_ref[j + 8, i, b].astype(F32)
                    window = win_ref[i, j * 16 : (j + 1) * 16].astype(F32)
                    out_ref[rows, :] = (own_ref[i, rows, :] + pieces + window).astype(BF16)

    @pl.when(even)
    def _():
        total(winn_ref, winp_ref)

    @pl.when(jnp.logical_not(even))
    def _():
        total(winp_ref, winn_ref)


def send(block, pairs):
    return lax.ppermute(block, "ctx", pairs)


def add(a, *others):
    total = a.astype(F32)
    for o in others:
        total = total + o.astype(F32)
    return total.astype(BF16)


def merge_stats(mine, other):
    sums, deltas = zip(*((a[:, :NH], a[:, NH:]) for a in (mine, other)))
    total = sums[0] + sums[1]
    inverse = jnp.where(total > 0, 1.0 / total, 0.0)
    delta = (sums[0] * inverse) * deltas[0] + (sums[1] * inverse) * deltas[1]
    return jnp.concatenate([total, delta], axis=1)


def per_device(queries, keys, values, grad_slab, plan, random_blocks):
    n_seg, n_ctx = lax.axis_size("segment"), lax.axis_size("ctx")
    rank = lax.axis_index("ctx").astype(jnp.int32)
    queries, keys, values, grad = queries[0], keys[0], values[0], grad_slab[0]
    width, q_width = keys.shape[2], queries.shape[2]
    half = q_width // 2
    info = jnp.concatenate([plan, rank[None]])
    halves = [list(range(8)), list(range(8, 16))]
    slots = jnp.concatenate(
        [jnp.zeros((n_ctx, 1), jnp.int32), random_blocks.reshape(n_ctx, 6)], axis=1
    )
    side = rank // 8
    table = lax.dynamic_slice_in_dim(slots, side * 8, 8, 0).reshape(56)
    table = jnp.concatenate([table, side[None]])

    def exchange(x):
        return lax.all_to_all(x, "ctx", 0, 0, tiled=True)

    def exchange_half(x):
        return lax.all_to_all(x, "ctx", 0, 0, tiled=True, axis_index_groups=halves)

    both = ("segment", "ctx")

    def flat(s, r):
        return (s % n_seg) * n_ctx + r

    own, send1, edge, q0, q1, g0, g1 = pack(info, keys, values, queries, grad)
    q1 = send(q1, [(0, 8)])
    g0 = lax.ppermute(g0, both, [(flat(s + 1, 0), flat(s, 0)) for s in range(n_seg)])
    g1 = lax.ppermute(g1, both, [(flat(s + 1, 0), flat(s, 8)) for s in range(n_seg)])
    got1 = exchange(send1)
    x = jnp.stack([jnp.where(rank == 0, q0, jnp.zeros((), BF16)) + q1, g0 + g1])
    swap = [(r, r ^ 1) for r in range(n_ctx)]
    ring = [(r, (r - 1 if r % 2 == 0 else r + 1) % n_ctx) for r in range(n_ctx)]
    partner, neighbour = send(own, swap), send(edge, ring)
    spread = [send(x, [(r, r + 2 * y) for r in (0, 8)]) for y in (1, 2, 3)]
    (send2,) = on_chip(select_kernel, "select", [stored((8, 2, 7, 16, width), BF16)], table, got1)
    x = after(x, send2) + sum(spread)
    x, send2, got1, grad, partner, neighbour = lax.optimization_barrier(
        (x, send2, got1, grad, partner, neighbour)
    )
    upstream = lax.ppermute(grad, "segment", [((s + 1) % n_seg, s) for s in range(n_seg)])
    got2 = exchange_half(send2)
    x = x + send(x, [(r, r + 1) for r in range(0, n_ctx, 2)])
    (stats,) = on_chip(stats_kernel, "row_stats", [stored((2, 8, BLK), F32)], info, x, got1)
    stats = merge_stats(stats, send(stats, swap))
    others = [
        send(stats, [(r, (r // 8) * 8 + (r + 2 * y) % 8) for r in range(n_ctx)]) for y in (1, 2, 3)
    ]
    got2, stats, *others = lax.optimization_barrier((got2, stats, *others))
    dq, down, winp, winn, send3 = attend(
        info, queries, upstream, own, partner, neighbour, got2
    )
    got3 = exchange_half(send3)
    stats, *others = lax.optimization_barrier((stats, *others, send3))[:4]
    stats = merge_stats(merge_stats(stats, others[1]), merge_stats(others[0], others[2]))
    part, row = on_chip(
        row_kernel,
        "row_grads",
        [stored((BLK, half), BF16), shape((16, 2, 2, 16, 2 * HD), F32)],
        info, x, got1, stats,
    )
    winp, winn = send(winp, swap), send(winn, ring)
    part = add(part, send(part, [(r + 1, r) for r in range(0, n_ctx, 2)]))
    near = [send(part, [(2 * y, 0), (8 + 2 * y, 1)]) for y in (1, 2, 3)]
    far = send(part, [(8, 1)])
    got3, winp, part, far, *near = lax.optimization_barrier((got3, winp, part, far, *near))

    (send4,) = on_chip(
        combine_kernel,
        "combine",
        [stored((16, 2, 2, 16, width), BF16)],
        table, got3, row,
        scratch=[pltpu.VMEM((16, 2, 2, 16, width), F32)],
    )
    got4 = exchange(send4)
    part = after(add(jnp.where(rank == 1, far, part), *near), send4)
    dq = place(info, [part, send(part, [(1, 0)])], dq)
    got4, dq = lax.optimization_barrier((got4, dq))
    dk, dv = on_chip(
        finish_kernel,
        "finish",
        [shape((2 * BLK, width), BF16)] * 2,
        info, down, winp, winn, got4,
    )
    return dq[None], dk[None], dv[None]


def solution(mesh):
    return jax.shard_map(
        per_device,
        mesh=mesh,
        in_specs=(
            P("segment", None, "ctx", None),
            P("segment", None, "ctx", None),
            P("segment", None, "ctx", None),
            P("segment", "ctx", None),
            P("segment"),
            P(),
        ),
        out_specs=(P("segment", "ctx", None), P("segment", "ctx", None), P("segment", "ctx", None)),
        check_vma=False,
    )
```

```python
import functools
import math

import jax
import jax.numpy as jnp
from jax import lax
from jax.experimental import pallas as pl
from jax.experimental.pallas import tpu as pltpu
from jax.sharding import PartitionSpec as P

HD = 128
BLK = 128
NH = 4
SCALE = HD**-0.5
EXP2_SCALE = SCALE * math.log2(math.e)
F32 = jnp.float32
BF16 = jnp.bfloat16
NT = (((1,), (1,)), ((), ()))
TN = (((0,), (0,)), ((), ()))
MIB = 2**20


def dot(a, b, dims=(((1,), (0,)), ((), ()))):
    return lax.dot_general(a, b, dims, preferred_element_type=F32)


def params(mib=8):
    return pltpu.CompilerParams(vmem_limit_bytes=mib * MIB)


def on_chip(kernel, name, out_shape, *operands, scratch=(), mib=8):
    vmem = pl.BlockSpec(memory_space=pltpu.VMEM)
    return pl.pallas_call(
        kernel,
        in_specs=[pl.BlockSpec(memory_space=pltpu.SMEM)] + [vmem] * (len(operands) - 1),
        out_specs=[vmem] * len(out_shape),
        out_shape=out_shape,
        scratch_shapes=list(scratch),
        compiler_params=params(mib),
        name=name,
    )(*operands)


def shape(dims, dtype):
    return jax.ShapeDtypeStruct(dims, dtype)


def stored(dims, dtype):
    return pltpu.HBM(dims, dtype)


def after(x, *others):
    return lax.optimization_barrier((x, *others))[0]


def pack_kernel(
    info_ref, k_ref, v_ref, q_ref, g_ref,
    kv_ref, send_ref, edge_ref, q0_ref, q1_ref, g0_ref, g1_ref,
):
    edge = pl.ds(pl.multiple_of(info_ref[1] % 2 * BLK, BLK), BLK)
    for i, ref in enumerate((k_ref, v_ref)):
        kv_ref[i] = ref[0]
        edge_ref[i] = ref[0, edge, :]
        for b in range(2):
            for j in range(8):
                piece = ref[0, b * BLK + j * 16 : b * BLK + (j + 1) * 16, :]
                send_ref[j, i, b] = piece
                send_ref[j + 8, i, b] = piece
    half = q0_ref.shape[1]
    q0_ref[...] = q_ref[0, :, :half]
    q1_ref[...] = q_ref[0, :, half:]
    g0_ref[...] = g_ref[:, :half]
    g1_ref[...] = g_ref[:, half:]


def pack(info, keys, values, queries, grad):
    width, q_width = keys.shape[2], queries.shape[2]
    spec = pl.BlockSpec((1, 2 * BLK, width), lambda i, info: (info[0], 0, 0))
    half = pl.BlockSpec((BLK, q_width // 2), lambda i, info: (0, 0))
    inputs = [pltpu.with_memory_space_constraint(a, pltpu.HBM) for a in (keys, values, queries, grad)]
    return pl.pallas_call(
        pack_kernel,
        grid_spec=pltpu.PrefetchScalarGridSpec(
            num_scalar_prefetch=1,
            grid=(1,),
            in_specs=[
                spec,
                spec,
                pl.BlockSpec((1, BLK, q_width), lambda i, info: (info[0], 0, 0)),
                pl.BlockSpec((BLK, q_width), lambda i, info: (0, 0)),
            ],
            out_specs=[
                pl.BlockSpec((2, 2 * BLK, width), lambda i, info: (0, 0, 0)),
                pl.BlockSpec((16, 2, 2, 16, width), lambda i, info: (0, 0, 0, 0, 0)),
                pl.BlockSpec((2, BLK, width), lambda i, info: (0, 0, 0)),
                *[half] * 4,
            ],
        ),
        out_shape=[
            stored((2, 2 * BLK, width), BF16),
            stored((16, 2, 2, 16, width), BF16),
            stored((2, BLK, width), BF16),
            *[stored((BLK, q_width // 2), BF16)] * 4,
        ],
        compiler_params=params(16),
        name="pack",
    )(info, *inputs)


def select_kernel(table_ref, got_ref, send_ref):
    for d in range(8):
        for s in range(7):
            block = table_ref[d * 7 + s]
            owner, which = block // 2, block % 2
            for i in range(2):
                send_ref[d, i, s] = got_ref[owner, i, which]


def combine_kernel(table_ref, got_ref, row_ref, send_ref, acc_ref):
    acc_ref[...] = jnp.zeros_like(acc_ref)
    acc_ref[:, :, :, :, columns(table_ref[56], 2 * HD)] = row_ref[...].astype(F32)
    for d in range(8):
        for s in range(7):
            block = table_ref[d * 7 + s]
            owner, which = block // 2, block % 2
            for i in range(2):
                acc_ref[owner, i, which] += got_ref[d, i, s].astype(F32)
    send_ref[...] = acc_ref[...].astype(BF16)


def heads_to_rows(cols):
    return jnp.concatenate([cols[:, h * HD : (h + 1) * HD] for h in range(NH)], axis=0)


def columns(g, width):
    return pl.ds(pl.multiple_of(g * width, width), width)


def attend_kernel(
    info_ref, q_ref, do_ref, own_ref, part_ref, nb_ref, rv_ref,
    dq_ref, down_ref, winp_ref, winn_ref, send_ref, wk_ref, zero_ref,
):
    rank = info_ref[1]
    even = rank % 2 == 0

    @pl.when(even)
    def _():
        wk_ref[0] = nb_ref[...]
        wk_ref[1] = part_ref[:, :BLK, :]

    @pl.when(jnp.logical_not(even))
    def _():
        wk_ref[0] = part_ref[:, BLK:, :]
        wk_ref[1] = nb_ref[...]

    def operands(n):
        rows = slice(n * BLK, (n + 1) * BLK)
        q, do = heads_to_rows(q_ref[0, rows, :]), heads_to_rows(do_ref[rows, :])

        def blocks(i):
            parts = [own_ref[i], wk_ref[n, i], rv_ref[:, i, 0].reshape(BLK, HD)]
            parts += [rv_ref[:, i, 1 + 3 * n + j].reshape(BLK, HD) for j in range(3)]
            return jnp.concatenate(parts, axis=0)

        return q, do, blocks(0), blocks(1)

    def exp_scores(n, q, do, k, v):
        e = jnp.exp2(dot(k, q, NT) * EXP2_SCALE)
        if n == 1:
            twice = jnp.logical_or(rank == 0, rank == 15)
            keep = jnp.where(twice, 0.0, 1.0).astype(F32)
            e = jnp.concatenate([e[: 3 * BLK], e[3 * BLK : 4 * BLK] * keep, e[4 * BLK :]], axis=0)
        return e

    def weights(e, q, do, k, v):
        p = e * (1.0 / jnp.sum(e, axis=0, keepdims=True))
        dp = dot(v, do, NT)
        delta = jnp.sum(p * dp, axis=0, keepdims=True)
        return p.astype(BF16), (p * (dp - delta)).astype(BF16)

    def grads(n, pb, ds, q, do, k, v):
        dqt = dot(k, ds, TN) * SCALE
        dq_ref[n * BLK : (n + 1) * BLK, :] = jnp.concatenate(
            [dqt[:, h * HD : (h + 1) * HD].T for h in range(NH)], axis=1
        ).astype(BF16)
        return dot(ds, q) * SCALE, dot(pb, do)

    def emit(n, grads):
        for i, grad in enumerate(grads):
            if n == 0:
                down_ref[i] = grad[: 2 * BLK]
                zero_ref[i] = grad[3 * BLK : 4 * BLK]
            else:
                down_ref[i] += grad[: 2 * BLK]
                total = zero_ref[i] + grad[3 * BLK : 4 * BLK]
                send_ref[:, i, 0] = total.astype(BF16).reshape(8, 16, HD)
            wk_ref[n, i] = grad[2 * BLK : 3 * BLK].astype(BF16)
            for j in range(3):
                got = grad[(4 + j) * BLK : (5 + j) * BLK].astype(BF16)
                send_ref[:, i, 1 + 3 * n + j] = got.reshape(8, 16, HD)

    given = [operands(n) for n in range(2)]
    scores = [exp_scores(n, *given[n]) for n in range(2)]
    shares = [weights(scores[n], *given[n]) for n in range(2)]
    first, second = (grads(n, *shares[n], *given[n]) for n in range(2))
    emit(0, [jnp.where(rank != 0, term, 0.0) for term in first])
    emit(1, second)

    @pl.when(even)
    def _():
        winn_ref[...] = wk_ref[0]
        winp_ref[...] = wk_ref[1]

    @pl.when(jnp.logical_not(even))
    def _():
        winp_ref[...] = wk_ref[0]
        winn_ref[...] = wk_ref[1]


def attend(info, queries, upstream, own, partner, neighbour, got):
    q_width, width = queries.shape[2], own.shape[2]
    kv_spec = pl.BlockSpec((2, 2 * BLK, HD), lambda g, info: (0, 0, g))
    win_spec = pl.BlockSpec((2, BLK, HD), lambda g, info: (0, 0, g))
    piece_spec = pl.BlockSpec((8, 2, 7, 16, HD), lambda g, info: (0, 0, 0, 0, g))
    row_spec = pl.BlockSpec((2 * BLK, NH * HD), lambda g, info: (0, g))
    return pl.pallas_call(
        attend_kernel,
        grid_spec=pltpu.PrefetchScalarGridSpec(
            num_scalar_prefetch=1,
            grid=(width // HD,),
            in_specs=[
                pl.BlockSpec((1, 2 * BLK, NH * HD), lambda g, info: (info[0], 0, g)),
                row_spec, kv_spec, kv_spec, win_spec, piece_spec,
            ],
            out_specs=[row_spec, kv_spec, win_spec, win_spec, piece_spec],
            scratch_shapes=[pltpu.VMEM((2, 2, BLK, HD), BF16), pltpu.VMEM((2, BLK, HD), F32)],
        ),
        out_shape=[
            stored((2 * BLK, q_width), BF16),
            stored((2, 2 * BLK, width), F32),
            stored((2, BLK, width), BF16),
            stored((2, BLK, width), BF16),
            stored((8, 2, 7, 16, width), BF16),
        ],
        compiler_params=params(28),
        cost_estimate=pl.CostEstimate(
            flops=10 * q_width * 14 * BLK * BLK, transcendentals=q_width * 14 * BLK, bytes_accessed=10 * MIB
        ),
        name="attend",
    )(
        info,
        *(
            pltpu.with_memory_space_constraint(a, pltpu.HBM)
            for a in (queries, upstream, own, partner, neighbour)
        ),
        got,
    )


def row_parts(info_ref, x_ref, got_ref, g):
    kc = columns(2 * (info_ref[1] // 8) + g, HD)
    qc = slice(g * NH * HD, (g + 1) * NH * HD)
    n_keys = got_ref.shape[0] * 2 * 16
    q, do = heads_to_rows(x_ref[0, :, qc]), heads_to_rows(x_ref[1, :, qc])
    return (q, do, *(got_ref[:, i, :, :, kc].reshape(n_keys, HD) for i in range(2)))


def stats_kernel(info_ref, x_ref, got_ref, out_ref):
    for g in range(2):
        q, do, k, v = row_parts(info_ref, x_ref, got_ref, g)
        e = jnp.exp2(dot(k, q, NT) * EXP2_SCALE)
        total = jnp.sum(e, axis=0, keepdims=True)
        inverse = jnp.where(total > 0, 1.0 / total, 0.0)
        delta = jnp.sum(e * inverse * dot(v, do, NT), axis=0, keepdims=True)
        rows = [a[:, h * BLK : (h + 1) * BLK] for a in (total, delta) for h in range(NH)]
        out_ref[g] = jnp.concatenate(rows, axis=0)


def row_kernel(info_ref, x_ref, got_ref, st_ref, dq_ref, down_ref):
    def lanes(a):
        return jnp.concatenate([a[h : h + 1] for h in range(NH)], axis=1)

    for g in range(2):
        q, do, k, v = row_parts(info_ref, x_ref, got_ref, g)
        inverse, mixed = 1.0 / st_ref[g, :NH, :], st_ref[g, NH:, :]
        p = jnp.exp2(dot(k, q, NT) * EXP2_SCALE) * lanes(inverse)
        pb = p.astype(BF16)
        ds = (p * (dot(v, do, NT) - lanes(mixed))).astype(BF16)
        dqt = dot(k, ds, TN) * SCALE
        dq_ref[:, g * NH * HD : (g + 1) * NH * HD] = jnp.concatenate(
            [dqt[:, h * HD : (h + 1) * HD].T for h in range(NH)], axis=1
        ).astype(BF16)
        kc = slice(g * HD, (g + 1) * HD)
        for i, grad in enumerate((dot(ds, q) * SCALE, dot(pb, do))):
            down_ref[:, i, :, :, kc] = grad.astype(BF16).reshape(16, 2, 16, HD)


def place_kernel(info_ref, *refs):
    *part_refs, dq_ref, out_ref = refs
    width = part_refs[0].shape[1]

    @pl.when(info_ref[1] == 0)
    def _():
        for h in range(2):
            out_ref[:, h * width : (h + 1) * width] = part_refs[h][...]

    @pl.when(info_ref[1] != 0)
    def _():
        out_ref[...] = dq_ref[...]


def place(info, parts, dq):
    top = pl.BlockSpec((BLK, dq.shape[1]), lambda i, info: (0, 0))
    piece = pl.BlockSpec(parts[0].shape, lambda i, info: (0, 0))
    return pl.pallas_call(
        place_kernel,
        grid_spec=pltpu.PrefetchScalarGridSpec(
            num_scalar_prefetch=1, grid=(1,), in_specs=[piece] * 2 + [top], out_specs=top
        ),
        out_shape=stored(dq.shape, BF16),
        input_output_aliases={3: 0},
        compiler_params=params(12),
        name="place",
    )(info, *parts, dq)


def finish_kernel(info_ref, own_ref, winp_ref, winn_ref, got_ref, dk_ref, dv_ref):
    even = info_ref[1] % 2 == 0

    def total(first_ref, second_ref):
        for i, out_ref in enumerate((dk_ref, dv_ref)):
            for b, win_ref in enumerate((first_ref, second_ref)):
                for j in range(8):
                    rows = slice(b * BLK + j * 16, b * BLK + (j + 1) * 16)
                    pieces = got_ref[j, i, b].astype(F32) + got_ref[j + 8, i, b].astype(F32)
                    window = win_ref[i, j * 16 : (j + 1) * 16].astype(F32)
                    out_ref[rows, :] = (own_ref[i, rows, :] + pieces + window).astype(BF16)

    @pl.when(even)
    def _():
        total(winn_ref, winp_ref)

    @pl.when(jnp.logical_not(even))
    def _():
        total(winp_ref, winn_ref)


def send(block, pairs):
    return lax.ppermute(block, "ctx", pairs)


def add(a, *others):
    total = a.astype(F32)
    for o in others:
        total = total + o.astype(F32)
    return total.astype(BF16)


def merge_stats(mine, other):
    sums, deltas = zip(*((a[:, :NH], a[:, NH:]) for a in (mine, other)))
    total = sums[0] + sums[1]
    inverse = jnp.where(total > 0, 1.0 / total, 0.0)
    delta = (sums[0] * inverse) * deltas[0] + (sums[1] * inverse) * deltas[1]
    return jnp.concatenate([total, delta], axis=1)


def per_device(queries, keys, values, grad_slab, plan, random_blocks):
    n_seg, n_ctx = lax.axis_size("segment"), lax.axis_size("ctx")
    rank = lax.axis_index("ctx").astype(jnp.int32)
    queries, keys, values, grad = queries[0], keys[0], values[0], grad_slab[0]
    width, q_width = keys.shape[2], queries.shape[2]
    half = q_width // 2
    info = jnp.concatenate([plan, rank[None]])
    halves = [list(range(8)), list(range(8, 16))]
    slots = jnp.concatenate(
        [jnp.zeros((n_ctx, 1), jnp.int32), random_blocks.reshape(n_ctx, 6)], axis=1
    )
    side = rank // 8
    table = lax.dynamic_slice_in_dim(slots, side * 8, 8, 0).reshape(56)
    table = jnp.concatenate([table, side[None]])

    def exchange(x):
        return lax.all_to_all(x, "ctx", 0, 0, tiled=True)

    def exchange_half(x):
        return lax.all_to_all(x, "ctx", 0, 0, tiled=True, axis_index_groups=halves)

    both = ("segment", "ctx")

    def flat(s, r):
        return (s % n_seg) * n_ctx + r

    own, send1, edge, q0, q1, g0, g1 = pack(info, keys, values, queries, grad)
    q1 = send(q1, [(0, 8)])
    g0 = lax.ppermute(g0, both, [(flat(s + 1, 0), flat(s, 0)) for s in range(n_seg)])
    g1 = lax.ppermute(g1, both, [(flat(s + 1, 0), flat(s, 8)) for s in range(n_seg)])
    got1 = exchange(send1)
    x = jnp.stack([jnp.where(rank == 0, q0, jnp.zeros((), BF16)) + q1, g0 + g1])
    swap = [(r, r ^ 1) for r in range(n_ctx)]
    ring = [(r, (r - 1 if r % 2 == 0 else r + 1) % n_ctx) for r in range(n_ctx)]
    partner, neighbour = send(own, swap), send(edge, ring)
    spread = [send(x, [(r, r + 2 * y) for r in (0, 8)]) for y in (1, 2, 3)]
    (send2,) = on_chip(select_kernel, "select", [stored((8, 2, 7, 16, width), BF16)], table, got1)
    x = after(x, send2) + sum(spread)
    x, send2, got1, grad, partner, neighbour = lax.optimization_barrier(
        (x, send2, got1, grad, partner, neighbour)
    )
    upstream = lax.ppermute(grad, "segment", [((s + 1) % n_seg, s) for s in range(n_seg)])
    got2 = exchange_half(send2)
    x = x + send(x, [(r, r + 1) for r in range(0, n_ctx, 2)])
    (stats,) = on_chip(stats_kernel, "row_stats", [stored((2, 8, BLK), F32)], info, x, got1)
    stats = merge_stats(stats, send(stats, swap))
    others = [
        send(stats, [(r, (r // 8) * 8 + (r + 2 * y) % 8) for r in range(n_ctx)]) for y in (1, 2, 3)
    ]
    got2, stats, *others = lax.optimization_barrier((got2, stats, *others))
    dq, down, winp, winn, send3 = attend(
        info, queries, upstream, own, partner, neighbour, got2
    )
    got3 = exchange_half(send3)
    stats, *others = lax.optimization_barrier((stats, *others, send3))[:4]
    stats = merge_stats(merge_stats(stats, others[1]), merge_stats(others[0], others[2]))
    part, row = on_chip(
        row_kernel,
        "row_grads",
        [stored((BLK, half), BF16), shape((16, 2, 2, 16, 2 * HD), BF16)],
        info, x, got1, stats,
    )
    winp, winn = send(winp, swap), send(winn, ring)
    part = add(part, send(part, [(r + 1, r) for r in range(0, n_ctx, 2)]))
    near = [send(part, [(2 * y, 0), (8 + 2 * y, 1)]) for y in (1, 2, 3)]
    far = send(part, [(8, 1)])
    got3, winp, part, far, *near = lax.optimization_barrier((got3, winp, part, far, *near))

    (send4,) = on_chip(
        combine_kernel,
        "combine",
        [stored((16, 2, 2, 16, width), BF16)],
        table, got3, row,
        scratch=[pltpu.VMEM((16, 2, 2, 16, width), F32)],
    )
    got4 = exchange(send4)
    part = after(add(jnp.where(rank == 1, far, part), *near), send4)
    dq = place(info, [part, send(part, [(1, 0)])], dq)
    got4, dq = lax.optimization_barrier((got4, dq))
    dk, dv = on_chip(
        finish_kernel,
        "finish",
        [shape((2 * BLK, width), BF16)] * 2,
        info, down, winp, winn, got4,
    )
    return dq[None], dk[None], dv[None]


def solution(mesh):
    return jax.shard_map(
        per_device,
        mesh=mesh,
        in_specs=(
            P("segment", None, "ctx", None),
            P("segment", None, "ctx", None),
            P("segment", None, "ctx", None),
            P("segment", "ctx", None),
            P("segment"),
            P(),
        ),
        out_specs=(P("segment", "ctx", None), P("segment", "ctx", None), P("segment", "ctx", None)),
        check_vma=False,
    )
```
